32 devices in a mesh: row: 8 (over z, x), col: 4 (over y, core).
Axes of the slice: x: 2, y: 2, z: 4, core: 2. Of those that a mesh axis runs over, the one named last changes fastest.
Arguments:
- off_blocks: bfloat16 [2048, 4, 96, 96], P(('row', 'col')), may hold values from -0.625 to 0.625
- neighbour: int32 [2048, 4], P(('row', 'col')), may hold values from 0 to 5
- active: int32 [2048, 4], P(('row', 'col')), may hold values 0 or 1
- diag_blocks: bfloat16 [2048, 96, 96], P(('row', 'col')), may hold values from -0.625 to 0.625
- diag_inverse: bfloat16 [2048, 96, 96], P(('row', 'col')), may hold values from -0.625 to 0.625
- tentative: bfloat16 [2048, 96, 96], P(('row', 'col')), may hold values from -0.21875 to 0.21875
- aggregate: int32 [2048], P(('row', 'col')), may hold values from 0 to 1
- owner_row: int32 [256, 1], P('row'), may hold values from 0 to 7; in each aligned block of 32 rows (0 to 31, 32 to 63, ...) at most 8 rows name the same one
- owner_group: int32 [256], P('row'), may hold values from 0 to 7
Outputs:
- coarse_blocks: float32 [64, 192, 192], P('row', 'col')
The draws below stay inside these ranges and needn't reach their ends.
Inputs may be any that keep to these rules, and one draw needn't show every extreme that they name: `owner_row`: among the 32 clusters of one row tile at most 8 have the same owner row, and exactly 8 do in some tile.
All inputs are finite; a program needn't handle non-finite values. No bound on the sum of `active` on one device may be relied on, other than what follows from the above.
Results may differ from the reference program's by a relative error of at most 0.006.
Values may be sent and summed in bfloat16 or wider, within the bound.
No kernel may reach another device: no remote copies, remote signals or barrier semaphores. Data moves between devices by JAX's collectives and lax.ppermute only.
A program may use at most 128 MiB of HBM per device.

```python
import math
import jax
import jax.numpy as jnp
import numpy as np
from jax import lax

B = 96
CW = 2
S = 4
RQ = 2
NQ = 32
G_DEV = 8
CAP = 8
NB = 2048
NQT = 256
N_ROW = 8
N_COL = 4


def touch_ends(values, key, smallest, top_value):
    shape = values.shape
    index_at = [jax.random.randint(jax.random.fold_in(key, axis), (), 0, shape[axis]) for axis in range(len(shape))]
    values = values.at[tuple(index_at)].set(smallest)
    longest = shape.index(max(shape))
    index_at[longest] = (index_at[longest] + 1) % shape[longest]
    return values.at[tuple(index_at)].set(top_value)


def shard_levels(rng, extent, split, smallest, largest):
    def one(axis_at, shards_of):
        heights = jax.random.uniform(jax.random.fold_in(jax.random.fold_in(rng, 6), axis_at), (shards_of,), jnp.float32, smallest / len(split), largest / len(split))
        return jnp.repeat(jnp.exp(heights), extent[axis_at] // shards_of).reshape((-1,) + (1,) * (len(extent) - axis_at - 1))

    factor_of = one(*split[0])
    for cut in split[1:]:
        factor_of = factor_of * one(*cut)
    return factor_of


def shared_out(rng, own, number, rows, count, top, most, skew):
    order = jax.random.permutation(rng, count)
    heavy_load, usual = portions_of(count, rows * top, most, skew, True), portions_of(count, rows * top, most, skew, False)
    places = jnp.arange(count)

    def named(lengths, offset_by):
        used = int((lengths > 0).sum())
        fixed = max(1, used // 4)
        shifted = fixed + (places - fixed + offset_by * (used - fixed)) % max(1, count - fixed)
        return jnp.zeros((count,), jnp.int32).at[order[jnp.where(places < fixed, places, shifted)]].set(jnp.asarray(lengths, jnp.int32))

    lengths = jnp.where(number % 4 == 0, named(heavy_load, number // 4), named(usual, number - number // 4 - 1))
    mixed = jax.random.permutation(jax.random.fold_in(own, 3), count)
    giver, receiver = mixed[0:count // 2 * 2:2], mixed[1:count // 2 * 2:2]
    margin = jnp.minimum(lengths[giver] - 1, most - lengths[receiver]) // 2
    margin = jnp.where((giver == order[0]) | (receiver == order[0]) | (lengths[receiver] == 0), 0, jnp.maximum(margin, 0))
    shifted = jax.random.randint(jax.random.fold_in(own, 4), (count // 2,), 0, 1 << 20) % (margin + 1)
    lengths = lengths.at[giver].add(-shifted).at[receiver].add(shifted)
    items = jnp.searchsorted(jnp.cumsum(lengths), jnp.arange(rows * top), side="right").astype(jnp.int32)
    table = items.reshape(top, rows).T
    table = table[jax.random.permutation(jax.random.fold_in(own, 1), rows)]
    offset_by = jax.random.randint(jax.random.fold_in(own, 2), (rows, 1), 0, top)
    return jnp.take_along_axis(table, (jnp.arange(top)[None, :] + offset_by) % top, axis=1)


def portions_of(number_of, total, limit, lean, full):
    weights = [(1 << 20) // math.isqrt(grade ** lean) + 1 for grade in range(1, number_of + 1)]
    largest = limit if full else min(limit, max(-(-total // number_of), total * weights[0] // sum(weights)))
    least = 1 if total - largest >= number_of - 1 else 0
    counts, spare = [largest] + [least] * (number_of - 1), total - largest - least * (number_of - 1)
    while spare > 0:
        movable = [i for i in range(1, number_of) if counts[i] < largest] or [i for i in range(1, number_of) if counts[i] < limit]
        mass, budget = sum([weights[i] for i in movable]), spare
        for i in movable:
            extra = min(limit - counts[i], max(1, budget * weights[i] // mass), spare)
            counts[i] = counts[i] + extra
            spare = spare - extra
    return np.array(counts)


def centred(rng, dims, deviation, limit, shards=(), kind=jnp.bfloat16):
    array = jax.random.normal(rng, dims, jnp.float32) * deviation
    if len(shards) > 0:
        array = shard_levels(rng, dims, shards, -0.22, 0.18) * array
    return jnp.clip(array, min=-limit, max=limit).astype(kind)


def setup_inputs(seed: int = 0) -> dict:
    splits = jax.random.split(jax.random.key(seed), 10)
    off_blocks = centred(splits[0], (NB, S, B, B), B ** -0.5, 0.625, ((0, 32),))
    neighbour = touch_ends(jax.random.randint(splits[1], (NB, S), 0, 3 * RQ), jax.random.fold_in(splits[1], 1), 0, (3 * RQ) - 1).astype(jnp.int32)
    active = touch_ends((jax.random.randint(splits[2], (NB, S), 0, 20) < 19).astype(jnp.int32), jax.random.fold_in(splits[2], 1), 0, 1)
    diag_blocks = centred(splits[3], (NB, B, B), B ** -0.5, 0.625, ((0, 32),))
    diag_inverse = centred(splits[4], (NB, B, B), B ** -0.5, 0.625, ((0, 32),))
    tentative = centred(splits[5], (NB, B, B), (8 * B) ** -0.5, 0.21875, ((0, 32),))
    aggregate = touch_ends(jax.random.randint(splits[6], (NB,), 0, CW), jax.random.fold_in(splits[6], 1), 0, CW - 1).astype(jnp.int32)
    owner_row_keys = jax.random.split(jax.random.fold_in(splits[7], 1), NQT // NQ)
    owner_row_turns = jax.random.permutation(jax.random.fold_in(splits[7], 3), NQT // NQ)
    owner_row = jax.vmap(lambda own, number: shared_out(jax.random.fold_in(splits[7], 2), own, number, NQ, N_ROW, 1, CAP, 2))(owner_row_keys, owner_row_turns).reshape((NQT, 1))
    owner_group = touch_ends(jax.random.randint(splits[8], (NQT,), 0, G_DEV), jax.random.fold_in(splits[8], 1), 0, G_DEV - 1).astype(jnp.int32)
    return dict(off_blocks=off_blocks, neighbour=neighbour, active=active, diag_blocks=diag_blocks, diag_inverse=diag_inverse, tentative=tentative, aggregate=aggregate, owner_row=owner_row, owner_group=owner_group)


OMEGA = 0.6


def widen(blocks, labels, window):
    onehot = (labels[..., None] == jnp.arange(window, dtype=jnp.int32)).astype(blocks.dtype)
    spread_out = blocks[..., :, None, :] * onehot[..., None, :, None]
    return spread_out.reshape(blocks.shape[:-1] + (window * blocks.shape[-1],))


def neighbour_index(near_slots, per_device):
    row_count = near_slots.shape[0]
    cluster_base = (jnp.arange(row_count, dtype=jnp.int32) // per_device) * per_device
    return ((near_slots // per_device) * row_count + cluster_base[:, None] + near_slots % per_device).astype(jnp.int32)


def apply_rows(diag_part, off_part, active_part, with_rim, near_index):
    row_count = diag_part.shape[0]
    own_rows = with_rim[row_count:2 * row_count].astype(jnp.float32)
    near_rows = jnp.take(with_rim, near_index, axis=0).astype(jnp.float32)
    weights = off_part.astype(jnp.float32) * active_part[:, :, None, None].astype(jnp.float32)
    summed = jnp.einsum('rij,rjw->riw', diag_part.astype(jnp.float32), own_rows)
    return summed + jnp.einsum('rsij,rsjw->riw', weights, near_rows)


def add_rim(field):
    return jnp.concatenate([jnp.roll(field, 1, axis=0), field, jnp.roll(field, -1, axis=0)], axis=1)


def tile_blocks(tile_arrays):
    off_t, near_t, active_t, diag_t, inverse_t, tent_t, aggregate_t = tile_arrays
    near_index = jax.vmap(lambda slots: neighbour_index(slots, RQ))(near_t)
    tent_wide = widen(tent_t, aggregate_t, CW)
    smooth_in = jax.vmap(apply_rows)(diag_t, off_t, active_t, add_rim(tent_wide), near_index).astype(jnp.bfloat16)
    correction = jnp.einsum('crij,crjw->criw', inverse_t.astype(jnp.float32), smooth_in.astype(jnp.float32))
    prolong = (tent_wide.astype(jnp.float32) - OMEGA * correction).astype(jnp.bfloat16)
    stiff_prol = jax.vmap(apply_rows)(diag_t, off_t, active_t, add_rim(prolong), near_index).astype(jnp.bfloat16)
    window = CW * B
    left_side = prolong.reshape(N_COL, NQ, RQ * B, window).transpose(1, 0, 2, 3).reshape(NQ, N_COL * RQ * B, window)
    right_side = stiff_prol.reshape(N_COL, NQ, RQ * B, window).transpose(1, 0, 2, 3).reshape(NQ, N_COL * RQ * B, window)
    return jnp.einsum('qmx,qmy->qxy', left_side.astype(jnp.float32), right_side.astype(jnp.float32))


def reference(off_blocks, neighbour, active, diag_blocks, diag_inverse, tentative, aggregate, owner_row, owner_group):
    def by_tiles(values):
        return values.reshape((N_ROW, N_COL, NQ * RQ) + values.shape[1:])

    tile_arrays = tuple(by_tiles(values) for values in (off_blocks, neighbour, active, diag_blocks, diag_inverse, tentative, aggregate))
    blocks = lax.map(tile_blocks, tile_arrays)
    blocks = blocks.reshape(N_ROW * NQ, CW * B, CW * B)
    target = (owner_row[:, 0] * G_DEV + owner_group).astype(jnp.int32)
    return jax.ops.segment_sum(blocks, target, num_segments=N_ROW * G_DEV)
```

```python
import functools

import jax
import jax.numpy as jnp
from jax import lax
from jax.experimental import pallas as pl
from jax.experimental.pallas import tpu as pltpu
from jax.sharding import PartitionSpec as P

CW = 2
RQ = 2
G_DEV = 8
OMEGA = 0.6

PARTS = 4
STEP = 2


VMEM = pl.BlockSpec(memory_space=pltpu.VMEM)
SMEM = pl.BlockSpec(memory_space=pltpu.SMEM)


def cost(flops, moved):
    return pl.CostEstimate(flops=int(flops), bytes_accessed=int(moved), transcendentals=0)


def pack_kernel(rows_ref, out_ref):
    per = rows_ref.shape[0] // out_ref.shape[0]
    width = rows_ref.shape[2]
    for m in range(out_ref.shape[0]):
        for j in range(per):
            out_ref[m, :, j * width : (j + 1) * width] = rows_ref[per * m + j]


def pack_rows(tentative, first, count):
    per = 2 * RQ
    _, high, width = tentative.shape
    step = STEP if count % STEP == 0 and first % STEP == 0 else 1
    return pl.pallas_call(
        pack_kernel,
        grid=(count // step,),
        in_specs=[pl.BlockSpec((per * step, high, width), lambda i: (i + first // step, 0, 0))],
        out_specs=pl.BlockSpec((step, high, per * width), lambda i: (i, 0, 0)),
        out_shape=jax.ShapeDtypeStruct((count, high, per * width), tentative.dtype),
        cost_estimate=cost(0, 5 * count * per * high * width),
    )(tentative)


def prolong_kernel(
    first, table, labels, off, diag, inverse, own, near_a, near_b, out, wide
):
    step = near_a.shape[0]
    slots, size = off.shape[1], off.shape[2]
    window = CW * size

    @pl.when(pl.program_id(0) == 0)
    def _():
        wide[3 * RQ] = jnp.zeros((size, window), wide.dtype)

    for m in range(step):
        for u in range(2):
            for k in range(RQ):
                j = u * RQ + k
                local = 2 * RQ * m + j
                row = 2 * RQ * (first + pl.program_id(0) * step + m) + j
                lanes = slice(j * size, (j + 1) * size)
                for side, block in enumerate(
                    (near_a[m, :, lanes], own[local], near_b[m, :, lanes])
                ):
                    label = labels[side, row]
                    for w in range(CW):
                        wide[side * RQ + k, :, w * size : (w + 1) * size] = jnp.where(
                            label == w, block, jnp.zeros_like(block)
                        )
            for k in range(RQ):
                j = u * RQ + k
                local = 2 * RQ * m + j
                row = 2 * RQ * (first + pl.program_id(0) * step + m) + j
                mine = wide[RQ + k]
                total = jnp.dot(diag[local], mine, preferred_element_type=jnp.float32)
                for s in range(slots):
                    total += jnp.dot(
                        off[local, s], wide[table[s, row]], preferred_element_type=jnp.float32
                    )
                change = jnp.dot(
                    inverse[local], total.astype(out.dtype), preferred_element_type=jnp.float32
                )
                out[2 * m + u, :, k * window : (k + 1) * window] = (
                    mine.astype(jnp.float32) - OMEGA * change
                ).astype(out.dtype)


def prolong_rows(table, labels, off, diag, inverse, tentative, near_a, near_b, first):
    per = 2 * RQ
    count, high, _ = near_a.shape
    slots, size = off.shape[1], off.shape[2]
    window = CW * size
    step = STEP if count % STEP == 0 and first % STEP == 0 else 1

    def rows(i):
        return (i + first // step, 0, 0)

    square = pl.BlockSpec((per * step, size, size), rows)
    packed = pl.BlockSpec((step, high, per * size), lambda i: (i, 0, 0))
    return pl.pallas_call(
        functools.partial(prolong_kernel, first),
        grid=(count // step,),
        in_specs=[
            SMEM,
            SMEM,
            pl.BlockSpec((per * step, slots, size, size), lambda i: rows(i) + (0,)),
            square,
            square,
            square,
            packed,
            packed,
        ],
        out_specs=pl.BlockSpec((2 * step, size, RQ * window), lambda i: (i, 0, 0)),
        out_shape=jax.ShapeDtypeStruct((2 * count, size, RQ * window), tentative.dtype),
        scratch_shapes=[pltpu.VMEM((3 * RQ + 1, size, window), tentative.dtype)],
        cost_estimate=cost(
            2 * count * per * (slots + 2) * size * size * window,
            2 * count * per * (slots + 7) * size * size,
        ),
    )(table, labels, off, diag, inverse, tentative, near_a, near_b)


def coarse_kernel(
    first, table, place, off, diag, own, near_a, near_b, keep, send, field, stiff, whole
):
    step = keep.shape[0]
    slots, size = off.shape[1], off.shape[2]
    window = CW * size
    halves, high = keep.shape[1], keep.shape[2]
    odd = place[0]

    @pl.when(pl.program_id(0) == 0)
    def _():
        field[3 * RQ] = jnp.zeros((size, window), field.dtype)

    for m in range(step):
        for u in range(2):
            for k in range(RQ):
                lanes = slice(k * window, (k + 1) * window)
                for side, source in enumerate((near_a, own, near_b)):
                    field[side * RQ + k] = source[2 * m + u, :, lanes]
            for k in range(RQ):
                j = u * RQ + k
                local = 2 * RQ * m + j
                row = 2 * RQ * (first + pl.program_id(0) * step + m) + j
                total = jnp.dot(diag[local], field[RQ + k], preferred_element_type=jnp.float32)
                for s in range(slots):
                    total += jnp.dot(
                        off[local, s], field[table[s, row]], preferred_element_type=jnp.float32
                    )
                stiff[k * size : (k + 1) * size, :] = total.astype(stiff.dtype)
            left = field[RQ : 2 * RQ].reshape(RQ * size, window)
            block = lax.dot_general(
                left, stiff[...], (((0,), (0,)), ((), ())), preferred_element_type=jnp.float32
            )
            for piece in range(2 * halves):
                whole[piece] = block[piece * high : (piece + 1) * high]
            lanes = slice(u * window, (u + 1) * window)
            for h in range(halves):
                keep[m, h, :, lanes] = whole[2 * h + odd]
                send[m, h, :, lanes] = whole[2 * h + 1 - odd].astype(send.dtype)


def coarse_rows(table, place, off, diag, own, near_a, near_b, first, columns):
    per = 2 * RQ
    count = own.shape[0] // 2
    slots, size = off.shape[1], off.shape[2]
    window = CW * size
    halves, high = columns // 2, window // columns
    step = STEP if count % STEP == 0 and first % STEP == 0 else 1

    def rows(i):
        return (i + first // step, 0, 0)

    packed = pl.BlockSpec((2 * step, size, RQ * window), lambda i: (i, 0, 0))
    result = pl.BlockSpec((step, halves, high, 2 * window), lambda i: (i, 0, 0, 0))
    shape = (count, halves, high, 2 * window)
    return pl.pallas_call(
        functools.partial(coarse_kernel, first),
        grid=(count // step,),
        in_specs=[
            SMEM,
            SMEM,
            pl.BlockSpec((per * step, slots, size, size), lambda i: rows(i) + (0,)),
            pl.BlockSpec((per * step, size, size), rows),
            packed,
            packed,
            packed,
        ],
        out_specs=[result, result],
        out_shape=[
            jax.ShapeDtypeStruct(shape, jnp.float32),
            jax.ShapeDtypeStruct(shape, own.dtype),
        ],
        scratch_shapes=[
            pltpu.VMEM((3 * RQ + 1, size, window), own.dtype),
            pltpu.VMEM((RQ * size, window), own.dtype),
            pltpu.VMEM((columns, high, window), jnp.float32),
        ],
        cost_estimate=cost(
            2 * count * per * (slots + 3) * size * size * window,
            2 * count * per * (slots + 12) * size * size,
        ),
    )(table, place, off, diag, own, near_a, near_b)


def group_kernel(parts, targets, place, *refs):
    sources = (refs[:parts], refs[parts : 2 * parts])
    keep, send, sums = refs[2 * parts :]
    high, window = sums.shape[1], sums.shape[2]
    groups = sums.shape[0] - 1
    low, odd = place[1], place[2]
    sums[...] = jnp.zeros_like(sums)
    for side in range(2):
        base = 0
        for source in sources[side]:

            def one(m, carry, source=source, base=base, side=side):
                for u in range(2):
                    target = targets[side, 2 * (base + m) + u]
                    owner, group = target // G_DEV, target % G_DEV
                    spot = jnp.where(owner % 2 == low, owner // 2 * G_DEV + group, groups)
                    sums[spot] += source[m, :, u * window : (u + 1) * window].astype(jnp.float32)
                return carry

            lax.fori_loop(0, source.shape[0], one, 0)
            base += source.shape[0]
    pairs = G_DEV // 2

    def place_one(i, carry):
        h, p = i // pairs, i % pairs
        for u in range(2):
            lanes = slice(u * window, (u + 1) * window)
            inner = 2 * p + u
            keep[h, p, :, lanes] = sums[(2 * h + odd) * G_DEV + inner]
            send[h, p, :, lanes] = sums[(2 * h + 1 - odd) * G_DEV + inner].astype(send.dtype)
        return carry

    lax.fori_loop(0, keep.shape[0] * pairs, place_one, 0)


def group_rows(targets, place, mine, theirs, rows):
    parts = len(mine)
    _, high, lanes = mine[0].shape
    shape = (rows // 4, G_DEV // 2, high, lanes)
    total = sum(part.shape[0] for part in mine)
    return pl.pallas_call(
        functools.partial(group_kernel, parts),
        in_specs=[SMEM, SMEM] + [VMEM] * (2 * parts),
        out_specs=[VMEM, VMEM],
        out_shape=[
            jax.ShapeDtypeStruct(shape, jnp.float32),
            jax.ShapeDtypeStruct(shape, mine[0].dtype),
        ],
        scratch_shapes=[pltpu.VMEM((rows // 2 * G_DEV + 1, high, lanes // 2), jnp.float32)],
        cost_estimate=cost(4 * total * high * lanes, 4 * total * high * lanes),
    )(targets, place, *mine, *theirs)


def finish_kernel(keep_ref, other_ref, out_ref):
    window = out_ref.shape[2]
    for p in range(keep_ref.shape[0]):
        total = keep_ref[p] + other_ref[p].astype(jnp.float32)
        for u in range(2):
            out_ref[2 * p + u] = total[:, u * window : (u + 1) * window]


def finish(keep, other):
    pairs, high, lanes = keep.shape
    return pl.pallas_call(
        finish_kernel,
        in_specs=[VMEM, VMEM],
        out_specs=VMEM,
        out_shape=jax.ShapeDtypeStruct((2 * pairs, high, lanes // 2), jnp.float32),
        cost_estimate=cost(pairs * high * lanes, 10 * pairs * high * lanes),
    )(keep, other)


def flip(count, bit):
    return [(i, i ^ bit) for i in range(count)]


def halve(keep, other, axis, bit, link):
    total = keep + other.astype(jnp.float32)
    shape = total.shape
    total = total.reshape(shape[:axis] + (shape[axis] // 2, 2) + shape[axis + 1 :])
    stay = lax.dynamic_index_in_dim(total, bit, axis + 1, keepdims=False)
    leave = lax.dynamic_index_in_dim(total, 1 - bit, axis + 1, keepdims=False)
    return stay, leave.astype(link)


def on_device(
    off_blocks,
    neighbour,
    active,
    diag_blocks,
    diag_inverse,
    tentative,
    aggregate,
    owner_row,
    owner_group,
):
    columns, rows = lax.axis_size("col"), lax.axis_size("row")
    col, row = lax.axis_index("col"), lax.axis_index("row")
    assert columns & (columns - 1) == 0 and columns >= 2
    assert rows & (rows - 1) == 0 and rows >= 4
    link = tentative.dtype
    groups = tentative.shape[0] // (2 * RQ)

    pair_a = flip(columns, 1)
    pair_b = [(i, (i + 1) % columns if i % 2 else (i - 1) % columns) for i in range(columns)]

    labels = jnp.stack(
        [
            lax.ppermute(aggregate, "col", pair_a),
            aggregate,
            lax.ppermute(aggregate, "col", pair_b),
        ]
    )
    targets = owner_row[:, 0] * G_DEV + owner_group
    targets = jnp.stack([targets, lax.ppermute(targets, "row", flip(rows, 1))])
    side = neighbour // RQ
    side = jnp.where(col % 2 == 0, 2 - side, side)
    table = jnp.where(active != 0, side * RQ + neighbour % RQ, 3 * RQ).T
    place = jnp.stack([col % 2, row % 2, row // 2 % 2])

    bounds = [groups * part // PARTS for part in range(PARTS + 1)]
    spans = list(zip(bounds[:-1], bounds[1:]))

    halos = []
    for low, high in spans:
        packed = pack_rows(tentative, low, high - low)
        halos.append(
            (lax.ppermute(packed, "col", pair_a), lax.ppermute(packed, "col", pair_b))
        )
    fields = []
    for (low, high), (near_a, near_b) in zip(spans, halos):
        field = prolong_rows(
            table, labels, off_blocks, diag_blocks, diag_inverse, tentative, near_a, near_b, low
        )
        fields.append(
            (field, lax.ppermute(field, "col", pair_a), lax.ppermute(field, "col", pair_b))
        )
    mine, theirs = [], []
    for (low, high), (field, near_a, near_b) in zip(spans, fields):
        keep, send = coarse_rows(
            table, place, off_blocks, diag_blocks, field, near_a, near_b, low, columns
        )
        bit = 1
        while bit < columns:
            other = lax.ppermute(send, "col", flip(columns, bit))
            bit *= 2
            if bit < columns:
                keep, send = halve(keep, other, 1, col // bit % 2, link)
        total = (keep + other.astype(jnp.float32)).astype(link)[:, 0]
        mine.append(total)
        theirs.append(lax.ppermute(total, "row", flip(rows, 1)))
    keep, send = group_rows(targets, place, mine, theirs, rows)
    bit = 2
    while bit < rows:
        other = lax.ppermute(send, "row", flip(rows, bit))
        bit *= 2
        if bit < rows:
            keep, send = halve(keep, other, 0, row // bit % 2, link)
    return finish(keep[0], other[0])


def solution(mesh):
    return jax.shard_map(
        on_device,
        mesh=mesh,
        in_specs=(
            P(("row", "col"), None, None, None),
            P(("row", "col"), None),
            P(("row", "col"), None),
            P(("row", "col"), None, None),
            P(("row", "col"), None, None),
            P(("row", "col"), None, None),
            P(("row", "col")),
            P("row", None),
            P("row"),
        ),
        out_specs=P("row", "col", None),
        check_vma=False,
    )
```

```python
import functools

import jax
import jax.numpy as jnp
from jax import lax
from jax.experimental import pallas as pl
from jax.experimental.pallas import tpu as pltpu
from jax.sharding import PartitionSpec as P


CW = 2
RQ = 2
G_DEV = 8
OMEGA = 0.6

EDGES = (0, 6, 12, 16)
STEP = 2


VMEM = pl.BlockSpec(memory_space=pltpu.VMEM)
SMEM = pl.BlockSpec(memory_space=pltpu.SMEM)
PARAMS = pltpu.CompilerParams(vmem_limit_bytes=67043328)


def step_of(first, count):
    return STEP if count % STEP == 0 and first % STEP == 0 else 1


def cost(flops, moved):
    return pl.CostEstimate(flops=int(flops), bytes_accessed=int(moved), transcendentals=0)


def pack_kernel(rows_ref, out_ref):
    per = rows_ref.shape[0] // out_ref.shape[0]
    width = rows_ref.shape[2]
    for m in range(out_ref.shape[0]):
        for j in range(per):
            out_ref[m, :, j * width : (j + 1) * width] = rows_ref[per * m + j]


def pack_rows(tentative, first, count):
    per = 2 * RQ
    _, high, width = tentative.shape
    step = step_of(first, count)
    return pl.pallas_call(
        pack_kernel,
        grid=(count // step,),
        in_specs=[pl.BlockSpec((per * step, high, width), lambda i: (i + first // step, 0, 0))],
        out_specs=pl.BlockSpec((step, high, per * width), lambda i: (i, 0, 0)),
        out_shape=jax.ShapeDtypeStruct((count, high, per * width), tentative.dtype),
        compiler_params=PARAMS,
        cost_estimate=cost(0, 5 * count * per * high * width),
    )(tentative)


def prolong_kernel(
    first, table, labels, off, diag, inverse, own, near_a, near_b, out, wide
):
    step = near_a.shape[0]
    slots, size = off.shape[1], off.shape[2]
    window = CW * size

    @pl.when(pl.program_id(0) == 0)
    def _():
        wide[3 * RQ] = jnp.zeros((size, window), wide.dtype)

    for m in range(step):
        for u in range(2):
            for k in range(RQ):
                j = u * RQ + k
                local = 2 * RQ * m + j
                row = 2 * RQ * (first + pl.program_id(0) * step + m) + j
                lanes = slice(j * size, (j + 1) * size)
                for side, block in enumerate(
                    (near_a[m, :, lanes], own[local], near_b[m, :, lanes])
                ):
                    label = labels[side, row]
                    for w in range(CW):
                        wide[side * RQ + k, :, w * size : (w + 1) * size] = jnp.where(
                            label == w, block, jnp.zeros_like(block)
                        )
            for k in range(RQ):
                j = u * RQ + k
                local = 2 * RQ * m + j
                row = 2 * RQ * (first + pl.program_id(0) * step + m) + j
                mine = wide[RQ + k]
                total = jnp.dot(diag[local], mine, preferred_element_type=jnp.float32)
                for s in range(slots):
                    total += jnp.dot(
                        off[local, s], wide[table[s, row]], preferred_element_type=jnp.float32
                    )
                change = jnp.dot(
                    inverse[local], total.astype(out.dtype), preferred_element_type=jnp.float32
                )
                out[2 * m + u, :, k * window : (k + 1) * window] = (
                    mine.astype(jnp.float32) - OMEGA * change
                ).astype(out.dtype)


def prolong_rows(table, labels, off, diag, inverse, tentative, near_a, near_b, first):
    per = 2 * RQ
    count, high, _ = near_a.shape
    slots, size = off.shape[1], off.shape[2]
    window = CW * size
    step = step_of(first, count)

    def rows(i):
        return (i + first // step, 0, 0)

    square = pl.BlockSpec((per * step, size, size), rows)
    packed = pl.BlockSpec((step, high, per * size), lambda i: (i, 0, 0))
    return pl.pallas_call(
        functools.partial(prolong_kernel, first),
        grid=(count // step,),
        in_specs=[
            SMEM,
            SMEM,
            pl.BlockSpec((per * step, slots, size, size), lambda i: rows(i) + (0,)),
            square,
            square,
            square,
            packed,
            packed,
        ],
        out_specs=pl.BlockSpec((2 * step, size, RQ * window), lambda i: (i, 0, 0)),
        out_shape=jax.ShapeDtypeStruct((2 * count, size, RQ * window), tentative.dtype),
        scratch_shapes=[pltpu.VMEM((3 * RQ + 1, size, window), tentative.dtype)],
        compiler_params=PARAMS,
        cost_estimate=cost(
            2 * count * per * (slots + 2) * size * size * window,
            2 * count * per * (slots + 7) * size * size,
        ),
    )(table, labels, off, diag, inverse, tentative, near_a, near_b)


def coarse_kernel(first, table, place, off, diag, own, near_a, near_b, keep, send, field, stiff, whole):
    step = keep.shape[1]
    slots, size = off.shape[1], off.shape[2]
    window = CW * size
    halves, high = keep.shape[0], keep.shape[2]
    col = place[0]

    @pl.when(pl.program_id(0) == 0)
    def _():
        field[3 * RQ] = jnp.zeros((size, window), field.dtype)

    for m in range(step):
        for u in range(2):
            for k in range(RQ):
                lanes = slice(k * window, (k + 1) * window)
                for side, source in enumerate((near_a, own, near_b)):
                    field[side * RQ + k] = source[2 * m + u, :, lanes]
            for k in range(RQ):
                j = u * RQ + k
                local = 2 * RQ * m + j
                row = 2 * RQ * (first + pl.program_id(0) * step + m) + j
                total = jnp.dot(diag[local], field[RQ + k], preferred_element_type=jnp.float32)
                for s in range(slots):
                    total += jnp.dot(
                        off[local, s], field[table[s, row]], preferred_element_type=jnp.float32
                    )
                stiff[k * size : (k + 1) * size, :] = total.astype(stiff.dtype)
            left = field[RQ : 2 * RQ].reshape(RQ * size, window)
            block = lax.dot_general(
                left, stiff[...], (((0,), (0,)), ((), ())), preferred_element_type=jnp.float32
            )
            for piece in range(2 * halves):
                whole[piece] = block[piece * high : (piece + 1) * high]
            lanes = slice(u * window, (u + 1) * window)
            for h in range(halves):
                keep[h, m, :, lanes] = whole[col ^ (2 * h)]
                send[h, m, :, lanes] = whole[col ^ (2 * h + 1)].astype(send.dtype)


def coarse_rows(table, place, off, diag, own, near_a, near_b, first, columns):
    per = 2 * RQ
    count = own.shape[0] // 2
    slots, size = off.shape[1], off.shape[2]
    window = CW * size
    halves, high = columns // 2, window // columns
    step = step_of(first, count)

    def rows(i):
        return (i + first // step, 0, 0)

    packed = pl.BlockSpec((2 * step, size, RQ * window), lambda i: (i, 0, 0))
    result = pl.BlockSpec((halves, step, high, 2 * window), lambda i: (0, i, 0, 0))
    shape = (halves, count, high, 2 * window)
    return pl.pallas_call(
        functools.partial(coarse_kernel, first),
        grid=(count // step,),
        in_specs=[
            SMEM,
            SMEM,
            pl.BlockSpec((per * step, slots, size, size), lambda i: rows(i) + (0,)),
            pl.BlockSpec((per * step, size, size), rows),
            packed,
            packed,
            packed,
        ],
        out_specs=[result, result],
        out_shape=[
            jax.ShapeDtypeStruct(shape, jnp.float32),
            jax.ShapeDtypeStruct(shape, own.dtype),
        ],
        scratch_shapes=[
            pltpu.VMEM((3 * RQ + 1, size, window), own.dtype),
            pltpu.VMEM((RQ * size, window), own.dtype),
            pltpu.VMEM((columns, high, window), jnp.float32),
        ],
        compiler_params=PARAMS,
        cost_estimate=cost(
            2 * count * per * (slots + 3) * size * size * window,
            2 * count * per * (slots + 12) * size * size,
        ),
    )(table, place, off, diag, own, near_a, near_b)


def add_groups(targets, place, sides, first, sums):
    groups = sums.shape[0] - 1
    window = sums.shape[2]
    row = place[1]
    for side, source in enumerate(sides):

        def one(m, carry, source=source, side=side):
            for u in range(2):
                target = targets[side, 2 * (first + m) + u]
                away = (target // G_DEV) ^ row
                spot = jnp.where(away % 2 == 0, away // 2 * G_DEV + target % G_DEV, groups)
                sums[spot] += source[m, :, u * window : (u + 1) * window].astype(jnp.float32)
            return carry

        count = source.shape[0]
        if count <= 4:
            for m in range(count):
                one(m, 0)
        else:
            lax.fori_loop(0, count, one, 0)


def gather_kernel(starts, targets, place, *refs):
    sums = refs[-1]
    sums[...] = jnp.zeros_like(sums)
    for part, first in enumerate(starts):
        add_groups(targets, place, refs[2 * part : 2 * part + 2], first, sums)


def gather_groups(targets, place, parts, starts, rows):
    _, high, lanes = parts[0][0].shape
    shape = (rows // 2 * G_DEV + 1, high, lanes // 2)
    flat = [array for pair in parts for array in pair]
    total = sum(array.size for array in flat)
    return pl.pallas_call(
        functools.partial(gather_kernel, starts),
        in_specs=[SMEM, SMEM] + [VMEM] * len(flat),
        out_specs=VMEM,
        out_shape=jax.ShapeDtypeStruct(shape, jnp.float32),
        compiler_params=PARAMS,
        cost_estimate=cost(total, 4 * total),
    )(targets, place, *flat)


def split_kernel(first, targets, place, early, mine, theirs, keep, send, sums):
    sums[...] = early[...]
    add_groups(targets, place, (mine, theirs), first, sums)
    window = sums.shape[2]
    for h in range(keep.shape[0]):
        for p in range(keep.shape[1]):
            for u in range(2):
                lanes = slice(u * window, (u + 1) * window)
                inner = 2 * p + u
                keep[h, p, :, lanes] = sums[2 * h * G_DEV + inner]
                send[h, p, :, lanes] = sums[(2 * h + 1) * G_DEV + inner].astype(send.dtype)


def split_groups(targets, place, early, mine, theirs, first, rows):
    _, high, lanes = mine.shape
    shape = (rows // 4, G_DEV // 2, high, lanes)
    return pl.pallas_call(
        functools.partial(split_kernel, first),
        in_specs=[SMEM, SMEM, VMEM, VMEM, VMEM],
        out_specs=[VMEM, VMEM],
        out_shape=[
            jax.ShapeDtypeStruct(shape, jnp.float32),
            jax.ShapeDtypeStruct(shape, mine.dtype),
        ],
        scratch_shapes=[pltpu.VMEM(early.shape, jnp.float32)],
        compiler_params=PARAMS,
        cost_estimate=cost(early.size, 10 * early.size),
    )(targets, place, early, mine, theirs)


def finish_kernel(keep_ref, *refs):
    others, out_ref = refs[:-1], refs[-1]
    window = out_ref.shape[2]
    for p in range(keep_ref.shape[1]):
        total = keep_ref[0, p]
        for other in others:
            total += other[0, p].astype(jnp.float32)
        for u in range(2):
            out_ref[2 * p + u] = total[:, u * window : (u + 1) * window]


def finish(keep, *others):
    _, pairs, high, lanes = keep.shape
    block = pl.BlockSpec((1, pairs, high, lanes), lambda i: (0, 0, 0, 0))
    return pl.pallas_call(
        finish_kernel,
        grid=(1,),
        in_specs=[block] * (1 + len(others)),
        out_specs=pl.BlockSpec((2 * pairs, high, lanes // 2), lambda i: (0, 0, 0)),
        out_shape=jax.ShapeDtypeStruct((2 * pairs, high, lanes // 2), jnp.float32),
        compiler_params=PARAMS,
        cost_estimate=cost(pairs * high * lanes, 10 * pairs * high * lanes),
    )(keep, *others)


def flip(count, bit):
    return [(i, i ^ bit) for i in range(count)]


def exchange(keep, send, axis, count, bit, link):
    terms = [keep]
    while True:
        terms.append(lax.ppermute(send, axis, flip(count, bit)))
        bit *= 2
        if bit == count:
            return terms
        send = sum(term[1::2].astype(jnp.float32) for term in terms).astype(link)
        terms = [term[0::2] for term in terms]


def on_device(
    off_blocks,
    neighbour,
    active,
    diag_blocks,
    diag_inverse,
    tentative,
    aggregate,
    owner_row,
    owner_group,
):
    columns, rows = lax.axis_size("col"), lax.axis_size("row")
    col, row = lax.axis_index("col"), lax.axis_index("row")
    assert columns & (columns - 1) == 0 and columns >= 2
    assert rows & (rows - 1) == 0 and rows >= 4
    link = tentative.dtype
    groups = tentative.shape[0] // (2 * RQ)

    pair_a = flip(columns, 1)
    pair_b = [(i, (i + 1) % columns if i % 2 else (i - 1) % columns) for i in range(columns)]

    bounds = [groups * edge // EDGES[-1] for edge in EDGES]
    spans = list(zip(bounds[:-1], bounds[1:]))

    def both(block):
        near_b = lax.ppermute(block, "col", pair_b)
        near_a = lax.ppermute(block, "col", pair_a)
        return near_a, near_b

    halos = []
    for low, high in spans:
        packed = pack_rows(tentative, low, high - low)
        halos.append(both(packed))
    label_a, label_b = both(aggregate)
    labels = jnp.stack([label_a, aggregate, label_b])
    targets = owner_row[:, 0] * G_DEV + owner_group
    other_targets = lax.ppermute(targets, "row", flip(rows, 1))
    targets = jnp.stack([targets, other_targets])
    side = neighbour // RQ
    side = jnp.where(col % 2 == 0, 2 - side, side)
    table = jnp.where(active != 0, side * RQ + neighbour % RQ, 3 * RQ).T
    place = jnp.stack([col, row])
    labels, targets, table, place = lax.optimization_barrier((labels, targets, table, place))

    fields = []
    for (low, high), (near_a, near_b) in zip(spans, halos):
        field = prolong_rows(
            table, labels, off_blocks, diag_blocks, diag_inverse, tentative, near_a, near_b, low
        )
        fields.append((field, *both(field)))
    parts = []
    for (low, high), (field, near_a, near_b) in zip(spans, fields):
        keep, send = coarse_rows(
            table, place, off_blocks, diag_blocks, field, near_a, near_b, low, columns
        )
        terms = exchange(keep, send, "col", columns, 1, link)
        total = sum(term[0].astype(jnp.float32) for term in terms).astype(link)
        other = lax.ppermute(total, "row", flip(rows, 1))
        parts.append((total, other))
    early = gather_groups(targets, place, parts[:-1], [low for low, _ in spans[:-1]], rows)
    keep, send = split_groups(targets, place, early, *parts[-1], spans[-1][0], rows)
    return finish(*exchange(keep, send, "row", rows, 2, link))


def solution(mesh):
    return jax.shard_map(
        on_device,
        mesh=mesh,
        in_specs=(
            P(("row", "col"), None, None, None),
            P(("row", "col"), None),
            P(("row", "col"), None),
            P(("row", "col"), None, None),
            P(("row", "col"), None, None),
            P(("row", "col"), None, None),
            P(("row", "col")),
            P("row", None),
            P("row"),
        ),
        out_specs=P("row", "col", None),
        check_vma=False,
    )
```

```python
import functools

import jax
import jax.numpy as jnp
from jax import lax
from jax.experimental import pallas as pl
from jax.experimental.pallas import tpu as pltpu
from jax.sharding import PartitionSpec as P


CW = 2
RQ = 2
G_DEV = 8
OMEGA = 0.6

EDGES = (0, 2, 8, 13, 16)
STEP = 2


VMEM = pl.BlockSpec(memory_space=pltpu.VMEM)
SMEM = pl.BlockSpec(memory_space=pltpu.SMEM)
PARAMS = pltpu.CompilerParams(vmem_limit_bytes=67043328)


def step_of(first, count):
    return STEP if count % STEP == 0 and first % STEP == 0 else 1


def cost(flops, moved):
    return pl.CostEstimate(flops=int(flops), bytes_accessed=int(moved), transcendentals=0)


def pack_kernel(rows_ref, out_ref):
    per = rows_ref.shape[0] // out_ref.shape[0]
    width = rows_ref.shape[2]
    for m in range(out_ref.shape[0]):
        for j in range(per):
            out_ref[m, :, j * width : (j + 1) * width] = rows_ref[per * m + j]


def pack_rows(tentative, first, count):
    per = 2 * RQ
    _, high, width = tentative.shape
    step = step_of(first, count)
    return pl.pallas_call(
        pack_kernel,
        grid=(count // step,),
        in_specs=[pl.BlockSpec((per * step, high, width), lambda i: (i + first // step, 0, 0))],
        out_specs=pl.BlockSpec((step, high, per * width), lambda i: (i, 0, 0)),
        out_shape=jax.ShapeDtypeStruct((count, high, per * width), tentative.dtype),
        compiler_params=PARAMS,
        cost_estimate=cost(0, 5 * count * per * high * width),
    )(tentative)


def prolong_kernel(
    first, table, labels, off, diag, inverse, own, near_a, near_b, out, wide
):
    step = near_a.shape[0]
    slots, size = off.shape[1], off.shape[2]
    window = CW * size

    @pl.when(pl.program_id(0) == 0)
    def _():
        wide[3 * RQ] = jnp.zeros((size, window), wide.dtype)

    for m in range(step):
        for u in range(2):
            for k in range(RQ):
                j = u * RQ + k
                local = 2 * RQ * m + j
                row = 2 * RQ * (first + pl.program_id(0) * step + m) + j
                lanes = slice(j * size, (j + 1) * size)
                for side, block in enumerate(
                    (near_a[m, :, lanes], own[local], near_b[m, :, lanes])
                ):
                    label = labels[side, row]
                    for w in range(CW):
                        wide[side * RQ + k, :, w * size : (w + 1) * size] = jnp.where(
                            label == w, block, jnp.zeros_like(block)
                        )
            for k in range(RQ):
                j = u * RQ + k
                local = 2 * RQ * m + j
                row = 2 * RQ * (first + pl.program_id(0) * step + m) + j
                mine = wide[RQ + k]
                total = jnp.dot(diag[local], mine, preferred_element_type=jnp.float32)
                for s in range(slots):
                    total += jnp.dot(
                        off[local, s], wide[table[s, row]], preferred_element_type=jnp.float32
                    )
                change = jnp.dot(
                    inverse[local], total.astype(out.dtype), preferred_element_type=jnp.float32
                )
                out[2 * m + u, :, k * window : (k + 1) * window] = (
                    mine.astype(jnp.float32) - OMEGA * change
                ).astype(out.dtype)


def prolong_rows(table, labels, off, diag, inverse, tentative, near_a, near_b, first):
    per = 2 * RQ
    count, high, _ = near_a.shape
    slots, size = off.shape[1], off.shape[2]
    window = CW * size
    step = step_of(first, count)

    def rows(i):
        return (i + first // step, 0, 0)

    square = pl.BlockSpec((per * step, size, size), rows)
    packed = pl.BlockSpec((step, high, per * size), lambda i: (i, 0, 0))
    return pl.pallas_call(
        functools.partial(prolong_kernel, first),
        grid=(count // step,),
        in_specs=[
            SMEM,
            SMEM,
            pl.BlockSpec((per * step, slots, size, size), lambda i: rows(i) + (0,)),
            square,
            square,
            square,
            packed,
            packed,
        ],
        out_specs=pl.BlockSpec((2 * step, size, RQ * window), lambda i: (i, 0, 0)),
        out_shape=jax.ShapeDtypeStruct((2 * count, size, RQ * window), tentative.dtype),
        scratch_shapes=[pltpu.VMEM((3 * RQ + 1, size, window), tentative.dtype)],
        compiler_params=PARAMS,
        cost_estimate=cost(
            2 * count * per * (slots + 2) * size * size * window,
            2 * count * per * (slots + 7) * size * size,
        ),
    )(table, labels, off, diag, inverse, tentative, near_a, near_b)


def coarse_kernel(first, table, place, off, diag, own, near_a, near_b, keep, send, field, stiff, whole):
    step = keep.shape[1]
    slots, size = off.shape[1], off.shape[2]
    window = CW * size
    halves, high = keep.shape[0], keep.shape[2]
    col = place[0]

    @pl.when(pl.program_id(0) == 0)
    def _():
        field[3 * RQ] = jnp.zeros((size, window), field.dtype)

    for m in range(step):
        for u in range(2):
            for k in range(RQ):
                lanes = slice(k * window, (k + 1) * window)
                for side, source in enumerate((near_a, own, near_b)):
                    field[side * RQ + k] = source[2 * m + u, :, lanes]
            for k in range(RQ):
                j = u * RQ + k
                local = 2 * RQ * m + j
                row = 2 * RQ * (first + pl.program_id(0) * step + m) + j
                total = jnp.dot(diag[local], field[RQ + k], preferred_element_type=jnp.float32)
                for s in range(slots):
                    total += jnp.dot(
                        off[local, s], field[table[s, row]], preferred_element_type=jnp.float32
                    )
                stiff[k * size : (k + 1) * size, :] = total.astype(stiff.dtype)
            left = field[RQ : 2 * RQ].reshape(RQ * size, window)
            block = lax.dot_general(
                left, stiff[...], (((0,), (0,)), ((), ())), preferred_element_type=jnp.float32
            )
            for piece in range(2 * halves):
                whole[piece] = block[piece * high : (piece + 1) * high]
            lanes = slice(u * window, (u + 1) * window)
            for h in range(halves):
                keep[h, m, :, lanes] = whole[col ^ (2 * h)]
                send[h, m, :, lanes] = whole[col ^ (2 * h + 1)].astype(send.dtype)


def coarse_rows(table, place, off, diag, own, near_a, near_b, first, columns):
    per = 2 * RQ
    count = own.shape[0] // 2
    slots, size = off.shape[1], off.shape[2]
    window = CW * size
    halves, high = columns // 2, window // columns
    step = step_of(first, count)

    def rows(i):
        return (i + first // step, 0, 0)

    packed = pl.BlockSpec((2 * step, size, RQ * window), lambda i: (i, 0, 0))
    result = pl.BlockSpec((halves, step, high, 2 * window), lambda i: (0, i, 0, 0))
    shape = (halves, count, high, 2 * window)
    return pl.pallas_call(
        functools.partial(coarse_kernel, first),
        grid=(count // step,),
        in_specs=[
            SMEM,
            SMEM,
            pl.BlockSpec((per * step, slots, size, size), lambda i: rows(i) + (0,)),
            pl.BlockSpec((per * step, size, size), rows),
            packed,
            packed,
            packed,
        ],
        out_specs=[result, result],
        out_shape=[
            jax.ShapeDtypeStruct(shape, jnp.float32),
            jax.ShapeDtypeStruct(shape, own.dtype),
        ],
        scratch_shapes=[
            pltpu.VMEM((3 * RQ + 1, size, window), own.dtype),
            pltpu.VMEM((RQ * size, window), own.dtype),
            pltpu.VMEM((columns, high, window), jnp.float32),
        ],
        compiler_params=PARAMS,
        cost_estimate=cost(
            2 * count * per * (slots + 3) * size * size * window,
            2 * count * per * (slots + 12) * size * size,
        ),
    )(table, place, off, diag, own, near_a, near_b)


def add_groups(targets, place, sides, first, sums):
    groups = sums.shape[0] - 1
    window = sums.shape[2]
    row = place[1]
    for side, source in enumerate(sides):

        def one(m, source=source, side=side):
            for u in range(2):
                target = targets[side, 2 * (first + m) + u]
                away = (target // G_DEV) ^ row
                spot = jnp.where(away % 2 == 0, away // 2 * G_DEV + target % G_DEV, groups)
                sums[spot] += source[m, :, u * window : (u + 1) * window].astype(jnp.float32)

        for m in range(source.shape[0]):
            one(m)


def gather_kernel(starts, targets, place, *refs):
    sums = refs[-1]
    sums[...] = jnp.zeros_like(sums)
    for part, first in enumerate(starts):
        add_groups(targets, place, refs[2 * part : 2 * part + 2], first, sums)


def gather_groups(targets, place, parts, starts, rows):
    _, high, lanes = parts[0][0].shape
    shape = (rows // 2 * G_DEV + 1, high, lanes // 2)
    flat = [array for pair in parts for array in pair]
    total = sum(array.size for array in flat)
    return pl.pallas_call(
        functools.partial(gather_kernel, starts),
        in_specs=[SMEM, SMEM] + [VMEM] * len(flat),
        out_specs=VMEM,
        out_shape=jax.ShapeDtypeStruct(shape, jnp.float32),
        compiler_params=PARAMS,
        cost_estimate=cost(total, 4 * total),
    )(targets, place, *flat)


def split_kernel(first, targets, place, early, mine, theirs, keep, odd, even, sums):
    sums[...] = early[...]
    add_groups(targets, place, (mine, theirs), first, sums)
    window = sums.shape[2]
    for h in range(keep.shape[0]):
        send = odd if h % 2 else even
        for p in range(keep.shape[1]):
            for u in range(2):
                lanes = slice(u * window, (u + 1) * window)
                inner = 2 * p + u
                keep[h, p, :, lanes] = sums[2 * h * G_DEV + inner]
                send[h // 2, p, :, lanes] = sums[(2 * h + 1) * G_DEV + inner].astype(send.dtype)


def split_groups(targets, place, early, mine, theirs, first, rows):
    _, high, lanes = mine.shape
    shape = (rows // 4, G_DEV // 2, high, lanes)
    half = jax.ShapeDtypeStruct((rows // 8,) + shape[1:], mine.dtype)
    return pl.pallas_call(
        functools.partial(split_kernel, first),
        in_specs=[SMEM, SMEM, VMEM, VMEM, VMEM],
        out_specs=[VMEM, VMEM, VMEM],
        out_shape=[jax.ShapeDtypeStruct(shape, jnp.float32), half, half],
        scratch_shapes=[pltpu.VMEM(early.shape, jnp.float32)],
        compiler_params=PARAMS,
        cost_estimate=cost(early.size, 10 * early.size),
    )(targets, place, early, mine, theirs)


def finish_kernel(keep_ref, *refs):
    others, out_ref = refs[:-1], refs[-1]
    window = out_ref.shape[2]
    for p in range(keep_ref.shape[1]):
        total = keep_ref[0, p]
        for other in others:
            total += other[0, p].astype(jnp.float32)
        for u in range(2):
            out_ref[2 * p + u] = total[:, u * window : (u + 1) * window]


def finish(keep, *others):
    _, pairs, high, lanes = keep.shape
    block = pl.BlockSpec((1, pairs, high, lanes), lambda i: (0, 0, 0, 0))
    return pl.pallas_call(
        finish_kernel,
        grid=(1,),
        in_specs=[block] * (1 + len(others)),
        out_specs=pl.BlockSpec((2 * pairs, high, lanes // 2), lambda i: (0, 0, 0)),
        out_shape=jax.ShapeDtypeStruct((2 * pairs, high, lanes // 2), jnp.float32),
        compiler_params=PARAMS,
        cost_estimate=cost(pairs * high * lanes, 10 * pairs * high * lanes),
    )(keep, *others)


def flip(count, bit):
    return [(i, i ^ bit) for i in range(count)]


def exchange(keep, send, axis, count, bit, link):
    terms = [keep]
    while True:
        route = flip(count, bit)
        if isinstance(send, tuple):
            odd = lax.ppermute(send[0], axis, route)
            even = lax.ppermute(send[1], axis, route)
        else:
            even = lax.ppermute(send, axis, route)
            if 2 * bit < count:
                even, odd = even[0::2], even[1::2]
        bit *= 2
        if bit == count:
            return terms + [even]
        send = sum(term[1::2].astype(jnp.float32) for term in terms)
        send = (send + odd.astype(jnp.float32)).astype(link)
        terms = [term[0::2] for term in terms] + [even]


def on_device(
    off_blocks,
    neighbour,
    active,
    diag_blocks,
    diag_inverse,
    tentative,
    aggregate,
    owner_row,
    owner_group,
):
    columns, rows = lax.axis_size("col"), lax.axis_size("row")
    col, row = lax.axis_index("col"), lax.axis_index("row")
    assert columns & (columns - 1) == 0 and columns >= 2
    assert rows & (rows - 1) == 0 and rows >= 8
    link = tentative.dtype
    groups = tentative.shape[0] // (2 * RQ)

    pair_a = flip(columns, 1)
    pair_b = [(i, (i + 1) % columns if i % 2 else (i - 1) % columns) for i in range(columns)]

    bounds = [groups * edge // EDGES[-1] for edge in EDGES]
    spans = list(zip(bounds[:-1], bounds[1:]))

    def both(block):
        near_b = lax.ppermute(block, "col", pair_b)
        near_a = lax.ppermute(block, "col", pair_a)
        return near_a, near_b

    halos = []
    for low, high in spans:
        packed = pack_rows(tentative, low, high - low)
        halos.append(both(packed))
    label_a, label_b = both(aggregate)
    labels = jnp.stack([label_a, aggregate, label_b])
    targets = owner_row[:, 0] * G_DEV + owner_group
    other_targets = lax.ppermute(targets, "row", flip(rows, 1))
    targets = jnp.stack([targets, other_targets])
    side = neighbour // RQ
    side = jnp.where(col % 2 == 0, 2 - side, side)
    table = jnp.where(active != 0, side * RQ + neighbour % RQ, 3 * RQ).T
    place = jnp.stack([col, row])
    labels, targets, table, place = lax.optimization_barrier((labels, targets, table, place))

    fields = []
    for (low, high), (near_a, near_b) in zip(spans, halos):
        field = prolong_rows(
            table, labels, off_blocks, diag_blocks, diag_inverse, tentative, near_a, near_b, low
        )
        fields.append((field, *both(field)))
    parts = []
    for (low, high), (field, near_a, near_b) in zip(spans, fields):
        keep, send = coarse_rows(
            table, place, off_blocks, diag_blocks, field, near_a, near_b, low, columns
        )
        terms = exchange(keep, send, "col", columns, 1, link)
        total = sum(term[0].astype(jnp.float32) for term in terms).astype(link)
        other = lax.ppermute(total, "row", flip(rows, 1))
        parts.append((total, other))
    early = gather_groups(targets, place, parts[:-1], [low for low, _ in spans[:-1]], rows)
    keep, *send = split_groups(targets, place, early, *parts[-1], spans[-1][0], rows)
    return finish(*exchange(keep, tuple(send), "row", rows, 2, link))


def solution(mesh):
    return jax.shard_map(
        on_device,
        mesh=mesh,
        in_specs=(
            P(("row", "col"), None, None, None),
            P(("row", "col"), None),
            P(("row", "col"), None),
            P(("row", "col"), None, None),
            P(("row", "col"), None, None),
            P(("row", "col"), None, None),
            P(("row", "col")),
            P("row", None),
            P("row"),
        ),
        out_specs=P("row", "col", None),
        check_vma=False,
    )
```

```python
import functools

import jax
import jax.numpy as jnp
from jax import lax
from jax.experimental import pallas as pl
from jax.experimental.pallas import tpu as pltpu
from jax.sharding import PartitionSpec as P


CW = 2
RQ = 2
G_DEV = 8
OMEGA = 0.6

EDGES = (0, 6, 12, 16)
STEP = 2


VMEM = pl.BlockSpec(memory_space=pltpu.VMEM)
SMEM = pl.BlockSpec(memory_space=pltpu.SMEM)
PARAMS = pltpu.CompilerParams(vmem_limit_bytes=67043328)


def step_of(first, count):
    return STEP if count % STEP == 0 and first % STEP == 0 else 1


def cost(flops, moved):
    return pl.CostEstimate(flops=int(flops), bytes_accessed=int(moved), transcendentals=0)


def pack_kernel(first, rows_ref, *outs):
    per = 2 * RQ
    width = rows_ref.shape[2]
    base = per * first
    for out in outs:
        for m in range(out.shape[0]):
            for j in range(per):
                out[m, :, j * width : (j + 1) * width] = rows_ref[base + per * m + j]
        base += per * out.shape[0]


def pack_rows(tentative, spans):
    per = 2 * RQ
    _, high, width = tentative.shape
    first, last = spans[0][0], spans[-1][1]
    whole = first % (last - first) == 0
    block = per * (last - first if whole else last)
    at = first // (last - first) if whole else 0
    counts = [stop - start for start, stop in spans]
    return pl.pallas_call(
        functools.partial(pack_kernel, 0 if whole else first),
        grid=(1,),
        in_specs=[pl.BlockSpec((block, high, width), lambda i: (at, 0, 0))],
        out_specs=[
            pl.BlockSpec((count, high, per * width), lambda i: (0, 0, 0)) for count in counts
        ],
        out_shape=[
            jax.ShapeDtypeStruct((count, high, per * width), tentative.dtype) for count in counts
        ],
        compiler_params=PARAMS,
        cost_estimate=cost(0, 5 * sum(counts) * per * high * width),
    )(tentative)


def prolong_kernel(first, table, labels, off, diag, inverse, own, near_a, near_b, out, *wides):
    step = near_a.shape[0]
    slots, size = off.shape[1], off.shape[2]
    window = CW * size
    start = 2 * RQ * (first + pl.program_id(0) * step)

    @pl.when(pl.program_id(0) == 0)
    def _():
        for wide in wides:
            wide[3 * RQ] = jnp.zeros((size, window), wide.dtype)

    for c, wide in enumerate(wides):
        m = c // 2
        for k in range(RQ):
            local = RQ * c + k
            j = local % (2 * RQ)
            lanes = slice(j * size, (j + 1) * size)
            for side, block in enumerate((near_a[m, :, lanes], own[local], near_b[m, :, lanes])):
                label = labels[side, start + local]
                for w in range(CW):
                    wide[side * RQ + k, :, w * size : (w + 1) * size] = jnp.where(
                        label == w, block, jnp.zeros_like(block)
                    )
    sums = []
    for c, wide in enumerate(wides):
        for k in range(RQ):
            local = RQ * c + k
            total = jnp.dot(diag[local], wide[RQ + k], preferred_element_type=jnp.float32)
            for s in range(slots):
                total += jnp.dot(
                    off[local, s],
                    wide[table[s, start + local]],
                    preferred_element_type=jnp.float32,
                )
            sums.append(total.astype(out.dtype))
    for c, wide in enumerate(wides):
        for k in range(RQ):
            local = RQ * c + k
            change = jnp.dot(inverse[local], sums[local], preferred_element_type=jnp.float32)
            out[c, :, k * window : (k + 1) * window] = (
                wide[RQ + k].astype(jnp.float32) - OMEGA * change
            ).astype(out.dtype)


def prolong_rows(table, labels, off, diag, inverse, tentative, near_a, near_b, first):
    per = 2 * RQ
    count, high, _ = near_a.shape
    slots, size = off.shape[1], off.shape[2]
    window = CW * size
    step = step_of(first, count)

    def rows(i):
        return (i + first // step, 0, 0)

    square = pl.BlockSpec((per * step, size, size), rows)
    packed = pl.BlockSpec((step, high, per * size), lambda i: (i, 0, 0))
    return pl.pallas_call(
        functools.partial(prolong_kernel, first),
        grid=(count // step,),
        in_specs=[
            SMEM,
            SMEM,
            pl.BlockSpec((per * step, slots, size, size), lambda i: rows(i) + (0,)),
            square,
            square,
            square,
            packed,
            packed,
        ],
        out_specs=pl.BlockSpec((2 * step, size, RQ * window), lambda i: (i, 0, 0)),
        out_shape=jax.ShapeDtypeStruct((2 * count, size, RQ * window), tentative.dtype),
        scratch_shapes=[pltpu.VMEM((3 * RQ + 1, size, window), tentative.dtype)] * (2 * step),
        compiler_params=PARAMS,
        cost_estimate=cost(
            2 * count * per * (slots + 2) * size * size * window,
            2 * count * per * (slots + 7) * size * size,
        ),
    )(table, labels, off, diag, inverse, tentative, near_a, near_b)


def coarse_kernel(first, table, place, off, diag, own, near_a, near_b, keep, send, *scratch):
    step = keep.shape[1]
    slots, size = off.shape[1], off.shape[2]
    window = CW * size
    halves, high = keep.shape[0], keep.shape[2]
    col = place[0]
    start = 2 * RQ * (first + pl.program_id(0) * step)
    fields, stiffs, wholes = (scratch[2 * step * i : 2 * step * (i + 1)] for i in range(3))

    @pl.when(pl.program_id(0) == 0)
    def _():
        for field in fields:
            field[3 * RQ] = jnp.zeros((size, window), field.dtype)

    for c, field in enumerate(fields):
        for k in range(RQ):
            lanes = slice(k * window, (k + 1) * window)
            for side, source in enumerate((near_a, own, near_b)):
                field[side * RQ + k] = source[c, :, lanes]
    for c, (field, stiff) in enumerate(zip(fields, stiffs)):
        for k in range(RQ):
            local = RQ * c + k
            total = jnp.dot(diag[local], field[RQ + k], preferred_element_type=jnp.float32)
            for s in range(slots):
                total += jnp.dot(
                    off[local, s],
                    field[table[s, start + local]],
                    preferred_element_type=jnp.float32,
                )
            stiff[k * size : (k + 1) * size, :] = total.astype(stiff.dtype)
    for field, stiff, whole in zip(fields, stiffs, wholes):
        left = field[RQ : 2 * RQ].reshape(RQ * size, window)
        block = lax.dot_general(
            left, stiff[...], (((0,), (0,)), ((), ())), preferred_element_type=jnp.float32
        )
        for piece in range(2 * halves):
            whole[piece] = block[piece * high : (piece + 1) * high]
    for c, whole in enumerate(wholes):
        lanes = slice(c % 2 * window, (c % 2 + 1) * window)
        for h in range(halves):
            keep[h, c // 2, :, lanes] = whole[col ^ (2 * h)]
            send[h, c // 2, :, lanes] = whole[col ^ (2 * h + 1)].astype(send.dtype)


def coarse_rows(table, place, off, diag, own, near_a, near_b, first, columns):
    per = 2 * RQ
    count = own.shape[0] // 2
    slots, size = off.shape[1], off.shape[2]
    window = CW * size
    halves, high = columns // 2, window // columns
    step = step_of(first, count)

    def rows(i):
        return (i + first // step, 0, 0)

    packed = pl.BlockSpec((2 * step, size, RQ * window), lambda i: (i, 0, 0))
    result = pl.BlockSpec((halves, step, high, 2 * window), lambda i: (0, i, 0, 0))
    shape = (halves, count, high, 2 * window)
    return pl.pallas_call(
        functools.partial(coarse_kernel, first),
        grid=(count // step,),
        in_specs=[
            SMEM,
            SMEM,
            pl.BlockSpec((per * step, slots, size, size), lambda i: rows(i) + (0,)),
            pl.BlockSpec((per * step, size, size), rows),
            packed,
            packed,
            packed,
        ],
        out_specs=[result, result],
        out_shape=[
            jax.ShapeDtypeStruct(shape, jnp.float32),
            jax.ShapeDtypeStruct(shape, own.dtype),
        ],
        scratch_shapes=[pltpu.VMEM((3 * RQ + 1, size, window), own.dtype)] * (2 * step)
        + [pltpu.VMEM((RQ * size, window), own.dtype)] * (2 * step)
        + [pltpu.VMEM((columns, high, window), jnp.float32)] * (2 * step),
        compiler_params=PARAMS,
        cost_estimate=cost(
            2 * count * per * (slots + 3) * size * size * window,
            2 * count * per * (slots + 12) * size * size,
        ),
    )(table, place, off, diag, own, near_a, near_b)


def add_groups(targets, place, sides, first, sums):
    groups = sums.shape[0] - 1
    window = sums.shape[2]
    row = place[1]
    for side, source in enumerate(sides):

        def one(m, source=source, side=side):
            for u in range(2):
                target = targets[side, 2 * (first + m) + u]
                away = (target // G_DEV) ^ row
                spot = jnp.where(away % 2 == 0, away // 2 * G_DEV + target % G_DEV, groups)
                sums[spot] += source[m, :, u * window : (u + 1) * window].astype(jnp.float32)

        for m in range(source.shape[0]):
            one(m)


def gather_kernel(starts, targets, place, *refs):
    sums = refs[-1]
    sums[...] = jnp.zeros_like(sums)
    for part, first in enumerate(starts):
        add_groups(targets, place, refs[2 * part : 2 * part + 2], first, sums)


def gather_groups(targets, place, parts, starts, rows):
    _, high, lanes = parts[0][0].shape
    shape = (rows // 2 * G_DEV + 1, high, lanes // 2)
    flat = [array for pair in parts for array in pair]
    total = sum(array.size for array in flat)
    return pl.pallas_call(
        functools.partial(gather_kernel, starts),
        in_specs=[SMEM, SMEM] + [VMEM] * len(flat),
        out_specs=VMEM,
        out_shape=jax.ShapeDtypeStruct(shape, jnp.float32),
        compiler_params=PARAMS,
        cost_estimate=cost(total, 4 * total),
    )(targets, place, *flat)


def split_kernel(first, targets, place, early, mine, theirs, keep, odd, even, sums):
    sums[...] = early[...]
    add_groups(targets, place, (mine, theirs), first, sums)
    window = sums.shape[2]
    for h in range(keep.shape[0]):
        send = odd if h % 2 else even
        for p in range(keep.shape[1]):
            for u in range(2):
                lanes = slice(u * window, (u + 1) * window)
                inner = 2 * p + u
                keep[h, p, :, lanes] = sums[2 * h * G_DEV + inner]
                send[h // 2, p, :, lanes] = sums[(2 * h + 1) * G_DEV + inner].astype(send.dtype)


def split_groups(targets, place, early, mine, theirs, first, rows):
    _, high, lanes = mine.shape
    shape = (rows // 4, G_DEV // 2, high, lanes)
    half = jax.ShapeDtypeStruct((rows // 8,) + shape[1:], mine.dtype)
    return pl.pallas_call(
        functools.partial(split_kernel, first),
        in_specs=[SMEM, SMEM, VMEM, VMEM, VMEM],
        out_specs=[VMEM, VMEM, VMEM],
        out_shape=[jax.ShapeDtypeStruct(shape, jnp.float32), half, half],
        scratch_shapes=[pltpu.VMEM(early.shape, jnp.float32)],
        compiler_params=PARAMS,
        cost_estimate=cost(early.size, 10 * early.size),
    )(targets, place, early, mine, theirs)


def finish_kernel(keep_ref, *refs):
    others, out_ref = refs[:-1], refs[-1]
    window = out_ref.shape[2]
    for p in range(keep_ref.shape[1]):
        total = keep_ref[0, p]
        for other in others:
            total += other[0, p].astype(jnp.float32)
        for u in range(2):
            out_ref[2 * p + u] = total[:, u * window : (u + 1) * window]


def finish(keep, *others):
    _, pairs, high, lanes = keep.shape
    block = pl.BlockSpec((1, pairs, high, lanes), lambda i: (0, 0, 0, 0))
    return pl.pallas_call(
        finish_kernel,
        grid=(1,),
        in_specs=[block] * (1 + len(others)),
        out_specs=pl.BlockSpec((2 * pairs, high, lanes // 2), lambda i: (0, 0, 0)),
        out_shape=jax.ShapeDtypeStruct((2 * pairs, high, lanes // 2), jnp.float32),
        compiler_params=PARAMS,
        cost_estimate=cost(pairs * high * lanes, 10 * pairs * high * lanes),
    )(keep, *others)


def flip(count, bit):
    return [(i, i ^ bit) for i in range(count)]


def exchange(keep, send, axis, count, bit, link):
    terms = [keep]
    while True:
        route = flip(count, bit)
        if isinstance(send, tuple):
            odd = lax.ppermute(send[0], axis, route)
            even = lax.ppermute(send[1], axis, route)
        else:
            even = lax.ppermute(send, axis, route)
            if 2 * bit < count:
                even, odd = even[0::2], even[1::2]
        bit *= 2
        if bit == count:
            return terms + [even]
        send = sum(term[1::2].astype(jnp.float32) for term in terms)
        send = (send + odd.astype(jnp.float32)).astype(link)
        terms = [term[0::2] for term in terms] + [even]


def on_device(
    off_blocks,
    neighbour,
    active,
    diag_blocks,
    diag_inverse,
    tentative,
    aggregate,
    owner_row,
    owner_group,
):
    columns, rows = lax.axis_size("col"), lax.axis_size("row")
    col, row = lax.axis_index("col"), lax.axis_index("row")
    assert columns & (columns - 1) == 0 and columns >= 2
    assert rows & (rows - 1) == 0 and rows >= 8
    link = tentative.dtype
    groups = tentative.shape[0] // (2 * RQ)

    pair_a = flip(columns, 1)
    pair_b = [(i, (i + 1) % columns if i % 2 else (i - 1) % columns) for i in range(columns)]

    bounds = [groups * edge // EDGES[-1] for edge in EDGES]
    spans = list(zip(bounds[:-1], bounds[1:]))

    def both(block):
        near_b = lax.ppermute(block, "col", pair_b)
        near_a = lax.ppermute(block, "col", pair_a)
        return near_a, near_b

    packed = list(pack_rows(tentative, spans[:1]))
    packed += pack_rows(tentative, spans[1:])
    halos = [both(block) for block in packed]
    label_a, label_b = both(aggregate)
    labels = jnp.stack([label_a, aggregate, label_b])
    targets = owner_row[:, 0] * G_DEV + owner_group
    other_targets = lax.ppermute(targets, "row", flip(rows, 1))
    targets = jnp.stack([targets, other_targets])
    side = neighbour // RQ
    side = jnp.where(col % 2 == 0, 2 - side, side)
    table = jnp.where(active != 0, side * RQ + neighbour % RQ, 3 * RQ).T
    place = jnp.stack([col, row])
    labels, targets, table, place = lax.optimization_barrier((labels, targets, table, place))

    fields = []
    for (low, high), (near_a, near_b) in zip(spans, halos):
        field = prolong_rows(
            table, labels, off_blocks, diag_blocks, diag_inverse, tentative, near_a, near_b, low
        )
        fields.append((field, *both(field)))
    parts = []
    for (low, high), (field, near_a, near_b) in zip(spans, fields):
        keep, send = coarse_rows(
            table, place, off_blocks, diag_blocks, field, near_a, near_b, low, columns
        )
        terms = exchange(keep, send, "col", columns, 1, link)
        total = sum(term[0].astype(jnp.float32) for term in terms).astype(link)
        other = lax.ppermute(total, "row", flip(rows, 1))
        parts.append((total, other))
    early = gather_groups(targets, place, parts[:-1], [low for low, _ in spans[:-1]], rows)
    keep, *send = split_groups(targets, place, early, *parts[-1], spans[-1][0], rows)
    return finish(*exchange(keep, tuple(send), "row", rows, 2, link))


def solution(mesh):
    return jax.shard_map(
        on_device,
        mesh=mesh,
        in_specs=(
            P(("row", "col"), None, None, None),
            P(("row", "col"), None),
            P(("row", "col"), None),
            P(("row", "col"), None, None),
            P(("row", "col"), None, None),
            P(("row", "col"), None, None),
            P(("row", "col")),
            P("row", None),
            P("row"),
        ),
        out_specs=P("row", "col", None),
        check_vma=False,
    )
```

```python
import functools

import jax
import jax.numpy as jnp
from jax import lax
from jax.experimental import pallas as pl
from jax.experimental.pallas import tpu as pltpu
from jax.sharding import PartitionSpec as P


CW = 2
RQ = 2
G_DEV = 8
OMEGA = 0.6

EDGES = (0, 8, 12, 16)
STEP = 2


VMEM = pl.BlockSpec(memory_space=pltpu.VMEM)
SMEM = pl.BlockSpec(memory_space=pltpu.SMEM)
PARAMS = pltpu.CompilerParams(vmem_limit_bytes=67043328)


def step_of(first, count):
    return STEP if count % STEP == 0 and first % STEP == 0 else 1


def cost(flops, moved):
    return pl.CostEstimate(flops=int(flops), bytes_accessed=int(moved), transcendentals=0)


def pack_kernel(first, rows_ref, *outs):
    per = 2 * RQ
    width = rows_ref.shape[2]
    base = per * first
    for out in outs:
        for m in range(out.shape[0]):
            for j in range(per):
                out[m, :, j * width : (j + 1) * width] = rows_ref[base + per * m + j]
        base += per * out.shape[0]


def pack_rows(tentative, spans):
    per = 2 * RQ
    _, high, width = tentative.shape
    first, last = spans[0][0], spans[-1][1]
    whole = first % (last - first) == 0
    block = per * (last - first if whole else last)
    at = first // (last - first) if whole else 0
    counts = [stop - start for start, stop in spans]
    return pl.pallas_call(
        functools.partial(pack_kernel, 0 if whole else first),
        grid=(1,),
        in_specs=[pl.BlockSpec((block, high, width), lambda i: (at, 0, 0))],
        out_specs=[
            pl.BlockSpec((count, high, per * width), lambda i: (0, 0, 0)) for count in counts
        ],
        out_shape=[
            jax.ShapeDtypeStruct((count, high, per * width), tentative.dtype) for count in counts
        ],
        compiler_params=PARAMS,
        cost_estimate=cost(0, 5 * sum(counts) * per * high * width),
    )(tentative)


def prolong_kernel(first, table, labels, off, diag, inverse, own, near_a, near_b, out, *wides):
    step = near_a.shape[0]
    slots, size = off.shape[1], off.shape[2]
    window = CW * size
    start = 2 * RQ * (first + pl.program_id(0) * step)

    @pl.when(pl.program_id(0) == 0)
    def _():
        for wide in wides:
            wide[3 * RQ] = jnp.zeros((size, window), wide.dtype)

    for c, wide in enumerate(wides):
        m = c // 2
        for k in range(RQ):
            local = RQ * c + k
            j = local % (2 * RQ)
            lanes = slice(j * size, (j + 1) * size)
            for side, block in enumerate((near_a[m, :, lanes], own[local], near_b[m, :, lanes])):
                label = labels[side, start + local]
                for w in range(CW):
                    wide[side * RQ + k, :, w * size : (w + 1) * size] = jnp.where(
                        label == w, block, jnp.zeros_like(block)
                    )
    sums = []
    for c, wide in enumerate(wides):
        for k in range(RQ):
            local = RQ * c + k
            total = jnp.dot(diag[local], wide[RQ + k], preferred_element_type=jnp.float32)
            for s in range(slots):
                total += jnp.dot(
                    off[local, s],
                    wide[table[s, start + local]],
                    preferred_element_type=jnp.float32,
                )
            sums.append(total.astype(out.dtype))
    for c, wide in enumerate(wides):
        for k in range(RQ):
            local = RQ * c + k
            change = jnp.dot(inverse[local], sums[local], preferred_element_type=jnp.float32)
            out[c, :, k * window : (k + 1) * window] = (
                wide[RQ + k].astype(jnp.float32) - OMEGA * change
            ).astype(out.dtype)


def prolong_rows(table, labels, off, diag, inverse, tentative, near_a, near_b, first):
    per = 2 * RQ
    count, high, _ = near_a.shape
    slots, size = off.shape[1], off.shape[2]
    window = CW * size
    step = step_of(first, count)

    def rows(i):
        return (i + first // step, 0, 0)

    square = pl.BlockSpec((per * step, size, size), rows)
    packed = pl.BlockSpec((step, high, per * size), lambda i: (i, 0, 0))
    return pl.pallas_call(
        functools.partial(prolong_kernel, first),
        grid=(count // step,),
        in_specs=[
            SMEM,
            SMEM,
            pl.BlockSpec((per * step, slots, size, size), lambda i: rows(i) + (0,)),
            square,
            square,
            square,
            packed,
            packed,
        ],
        out_specs=pl.BlockSpec((2 * step, size, RQ * window), lambda i: (i, 0, 0)),
        out_shape=jax.ShapeDtypeStruct((2 * count, size, RQ * window), tentative.dtype),
        scratch_shapes=[pltpu.VMEM((3 * RQ + 1, size, window), tentative.dtype)] * (2 * step),
        compiler_params=PARAMS,
        cost_estimate=cost(
            2 * count * per * (slots + 2) * size * size * window,
            2 * count * per * (slots + 7) * size * size,
        ),
    )(table, labels, off, diag, inverse, tentative, near_a, near_b)


def coarse_kernel(first, table, place, off, diag, own, near_a, near_b, keep, send, *scratch):
    step = keep.shape[1]
    slots, size = off.shape[1], off.shape[2]
    window = CW * size
    halves, high = keep.shape[0], keep.shape[2]
    col = place[0]
    start = 2 * RQ * (first + pl.program_id(0) * step)
    fields, stiffs, wholes = (scratch[2 * step * i : 2 * step * (i + 1)] for i in range(3))

    @pl.when(pl.program_id(0) == 0)
    def _():
        for field in fields:
            field[3 * RQ] = jnp.zeros((size, window), field.dtype)

    for c, field in enumerate(fields):
        for k in range(RQ):
            lanes = slice(k * window, (k + 1) * window)
            for side, source in enumerate((near_a, own, near_b)):
                field[side * RQ + k] = source[c, :, lanes]
    for c, (field, stiff) in enumerate(zip(fields, stiffs)):
        for k in range(RQ):
            local = RQ * c + k
            total = jnp.dot(diag[local], field[RQ + k], preferred_element_type=jnp.float32)
            for s in range(slots):
                total += jnp.dot(
                    off[local, s],
                    field[table[s, start + local]],
                    preferred_element_type=jnp.float32,
                )
            stiff[k * size : (k + 1) * size, :] = total.astype(stiff.dtype)
    for field, stiff, whole in zip(fields, stiffs, wholes):
        left = field[RQ : 2 * RQ].reshape(RQ * size, window)
        block = lax.dot_general(
            left, stiff[...], (((0,), (0,)), ((), ())), preferred_element_type=jnp.float32
        )
        for piece in range(2 * halves):
            whole[piece] = block[piece * high : (piece + 1) * high]
    for c, whole in enumerate(wholes):
        lanes = slice(c % 2 * window, (c % 2 + 1) * window)
        for h in range(halves):
            keep[h, c // 2, :, lanes] = whole[col ^ (2 * h)]
            send[h, c // 2, :, lanes] = whole[col ^ (2 * h + 1)].astype(send.dtype)


def coarse_rows(table, place, off, diag, own, near_a, near_b, first, columns):
    per = 2 * RQ
    count = own.shape[0] // 2
    slots, size = off.shape[1], off.shape[2]
    window = CW * size
    halves, high = columns // 2, window // columns
    step = step_of(first, count)

    def rows(i):
        return (i + first // step, 0, 0)

    packed = pl.BlockSpec((2 * step, size, RQ * window), lambda i: (i, 0, 0))
    result = pl.BlockSpec((halves, step, high, 2 * window), lambda i: (0, i, 0, 0))
    shape = (halves, count, high, 2 * window)
    return pl.pallas_call(
        functools.partial(coarse_kernel, first),
        grid=(count // step,),
        in_specs=[
            SMEM,
            SMEM,
            pl.BlockSpec((per * step, slots, size, size), lambda i: rows(i) + (0,)),
            pl.BlockSpec((per * step, size, size), rows),
            packed,
            packed,
            packed,
        ],
        out_specs=[result, result],
        out_shape=[
            jax.ShapeDtypeStruct(shape, jnp.float32),
            jax.ShapeDtypeStruct(shape, own.dtype),
        ],
        scratch_shapes=[pltpu.VMEM((3 * RQ + 1, size, window), own.dtype)] * (2 * step)
        + [pltpu.VMEM((RQ * size, window), own.dtype)] * (2 * step)
        + [pltpu.VMEM((columns, high, window), jnp.float32)] * (2 * step),
        compiler_params=PARAMS,
        cost_estimate=cost(
            2 * count * per * (slots + 3) * size * size * window,
            2 * count * per * (slots + 12) * size * size,
        ),
    )(table, place, off, diag, own, near_a, near_b)


def add_groups(targets, place, sides, first, sums):
    groups = sums.shape[0] - 1
    window = sums.shape[2]
    row = place[1]
    for side, source in enumerate(sides):

        def one(m, source=source, side=side):
            for u in range(2):
                target = targets[side, 2 * (first + m) + u]
                away = (target // G_DEV) ^ row
                spot = jnp.where(away % 2 == 0, away // 2 * G_DEV + target % G_DEV, groups)
                sums[spot] += source[m, :, u * window : (u + 1) * window].astype(jnp.float32)

        for m in range(source.shape[0]):
            one(m)


def gather_kernel(starts, targets, place, *refs):
    sums = refs[-1]
    sums[...] = jnp.zeros_like(sums)
    for part, first in enumerate(starts):
        add_groups(targets, place, refs[2 * part : 2 * part + 2], first, sums)


def gather_groups(targets, place, parts, starts, rows):
    _, high, lanes = parts[0][0].shape
    shape = (rows // 2 * G_DEV + 1, high, lanes // 2)
    flat = [array for pair in parts for array in pair]
    total = sum(array.size for array in flat)
    return pl.pallas_call(
        functools.partial(gather_kernel, starts),
        in_specs=[SMEM, SMEM] + [VMEM] * len(flat),
        out_specs=VMEM,
        out_shape=jax.ShapeDtypeStruct(shape, jnp.float32),
        compiler_params=PARAMS,
        cost_estimate=cost(total, 4 * total),
    )(targets, place, *flat)


def split_kernel(first, targets, place, early, mine, theirs, keep, odd, even, sums):
    sums[...] = early[...]
    add_groups(targets, place, (mine, theirs), first, sums)
    window = sums.shape[2]
    for h in range(keep.shape[0]):
        send = odd if h % 2 else even
        for p in range(keep.shape[1]):
            for u in range(2):
                lanes = slice(u * window, (u + 1) * window)
                inner = 2 * p + u
                keep[h, p, :, lanes] = sums[2 * h * G_DEV + inner]
                send[h // 2, p, :, lanes] = sums[(2 * h + 1) * G_DEV + inner].astype(send.dtype)


def split_groups(targets, place, early, mine, theirs, first, rows):
    _, high, lanes = mine.shape
    shape = (rows // 4, G_DEV // 2, high, lanes)
    half = jax.ShapeDtypeStruct((rows // 8,) + shape[1:], mine.dtype)
    return pl.pallas_call(
        functools.partial(split_kernel, first),
        in_specs=[SMEM, SMEM, VMEM, VMEM, VMEM],
        out_specs=[VMEM, VMEM, VMEM],
        out_shape=[jax.ShapeDtypeStruct(shape, jnp.float32), half, half],
        scratch_shapes=[pltpu.VMEM(early.shape, jnp.float32)],
        compiler_params=PARAMS,
        cost_estimate=cost(early.size, 10 * early.size),
    )(targets, place, early, mine, theirs)


def finish_kernel(keep_ref, *refs):
    others, out_ref = refs[:-1], refs[-1]
    window = out_ref.shape[2]
    for p in range(keep_ref.shape[1]):
        total = keep_ref[0, p]
        for other in others:
            total += other[0, p].astype(jnp.float32)
        for u in range(2):
            out_ref[2 * p + u] = total[:, u * window : (u + 1) * window]


def finish(keep, *others):
    _, pairs, high, lanes = keep.shape
    block = pl.BlockSpec((1, pairs, high, lanes), lambda i: (0, 0, 0, 0))
    return pl.pallas_call(
        finish_kernel,
        grid=(1,),
        in_specs=[block] * (1 + len(others)),
        out_specs=pl.BlockSpec((2 * pairs, high, lanes // 2), lambda i: (0, 0, 0)),
        out_shape=jax.ShapeDtypeStruct((2 * pairs, high, lanes // 2), jnp.float32),
        compiler_params=PARAMS,
        cost_estimate=cost(pairs * high * lanes, 10 * pairs * high * lanes),
    )(keep, *others)


def flip(count, bit):
    return [(i, i ^ bit) for i in range(count)]


def exchange(keep, send, axis, count, bit, link):
    terms = [(keep, 1)]
    while True:
        route = flip(count, bit)
        if isinstance(send, tuple):
            odd = lax.ppermute(send[0], axis, route)
            arrived = (lax.ppermute(send[1], axis, route), 1)
        else:
            arrived = (lax.ppermute(send, axis, route), 2)
            odd = arrived[0][1::2]
        bit *= 2
        if bit == count:
            return [term for term, _ in terms] + [arrived[0]]
        leave = sum(term[stride :: 2 * stride].astype(jnp.float32) for term, stride in terms)
        send = (leave + odd.astype(jnp.float32)).astype(link)
        terms = [(term, 2 * stride) for term, stride in terms] + [arrived]


def on_device(
    off_blocks,
    neighbour,
    active,
    diag_blocks,
    diag_inverse,
    tentative,
    aggregate,
    owner_row,
    owner_group,
):
    columns, rows = lax.axis_size("col"), lax.axis_size("row")
    col, row = lax.axis_index("col"), lax.axis_index("row")
    assert columns & (columns - 1) == 0 and columns >= 2
    assert rows & (rows - 1) == 0 and rows >= 8
    link = tentative.dtype
    groups = tentative.shape[0] // (2 * RQ)

    pair_a = flip(columns, 1)
    pair_b = [(i, (i + 1) % columns if i % 2 else (i - 1) % columns) for i in range(columns)]

    bounds = [groups * edge // EDGES[-1] for edge in EDGES]
    spans = list(zip(bounds[:-1], bounds[1:]))

    def both(block):
        near_b = lax.ppermute(block, "col", pair_b)
        near_a = lax.ppermute(block, "col", pair_a)
        return near_a, near_b

    packed = list(pack_rows(tentative, spans[:1]))
    packed += pack_rows(tentative, spans[1:])
    halos = [both(block) for block in packed]
    label_a, label_b = both(aggregate)
    labels = jnp.stack([label_a, aggregate, label_b])
    targets = owner_row[:, 0] * G_DEV + owner_group
    other_targets = lax.ppermute(targets, "row", flip(rows, 1))
    targets = jnp.stack([targets, other_targets])
    side = neighbour // RQ
    side = jnp.where(col % 2 == 0, 2 - side, side)
    table = jnp.where(active != 0, side * RQ + neighbour % RQ, 3 * RQ).T
    place = jnp.stack([col, row])
    labels, targets, table, place = lax.optimization_barrier((labels, targets, table, place))

    fields = []
    for (low, high), (near_a, near_b) in zip(spans, halos):
        field = prolong_rows(
            table, labels, off_blocks, diag_blocks, diag_inverse, tentative, near_a, near_b, low
        )
        fields.append((field, *both(field)))
    parts = []
    for (low, high), (field, near_a, near_b) in zip(spans, fields):
        keep, send = coarse_rows(
            table, place, off_blocks, diag_blocks, field, near_a, near_b, low, columns
        )
        terms = exchange(keep, send, "col", columns, 1, link)
        total = sum(term[0].astype(jnp.float32) for term in terms).astype(link)
        other = lax.ppermute(total, "row", flip(rows, 1))
        parts.append((total, other))
    early = gather_groups(targets, place, parts[:-1], [low for low, _ in spans[:-1]], rows)
    keep, *send = split_groups(targets, place, early, *parts[-1], spans[-1][0], rows)
    return finish(*exchange(keep, tuple(send), "row", rows, 2, link))


def solution(mesh):
    return jax.shard_map(
        on_device,
        mesh=mesh,
        in_specs=(
            P(("row", "col"), None, None, None),
            P(("row", "col"), None),
            P(("row", "col"), None),
            P(("row", "col"), None, None),
            P(("row", "col"), None, None),
            P(("row", "col"), None, None),
            P(("row", "col")),
            P("row", None),
            P("row"),
        ),
        out_specs=P("row", "col", None),
        check_vma=False,
    )
```

```python
import functools

import jax
import jax.numpy as jnp
from jax import lax
from jax.experimental import pallas as pl
from jax.experimental.pallas import tpu as pltpu
from jax.sharding import PartitionSpec as P


CW = 2
RQ = 2
G_DEV = 8
OMEGA = 0.6

EDGES = (0, 4, 12, 16)
STEP = 2


VMEM = pl.BlockSpec(memory_space=pltpu.VMEM)
SMEM = pl.BlockSpec(memory_space=pltpu.SMEM)
ANY = pl.BlockSpec(memory_space=pl.ANY)
SMALL = pltpu.CompilerParams(vmem_limit_bytes=50331648)
PARAMS = pltpu.CompilerParams(vmem_limit_bytes=67043328)


def step_of(first, count):
    return STEP if count % STEP == 0 and first % STEP == 0 else 1


def cost(flops, moved):
    return pl.CostEstimate(flops=int(flops), bytes_accessed=int(moved), transcendentals=0)


def pack_kernel(first, rows_ref, *outs):
    per = 2 * RQ
    width = rows_ref.shape[2]
    base = per * first
    for out in outs:
        for m in range(out.shape[0]):
            for j in range(per):
                out[m, :, j * width : (j + 1) * width] = rows_ref[base + per * m + j]
        base += per * out.shape[0]


def pack_rows(tentative, spans):
    per = 2 * RQ
    _, high, width = tentative.shape
    first, last = spans[0][0], spans[-1][1]
    whole = first % (last - first) == 0
    block = per * (last - first if whole else last)
    at = first // (last - first) if whole else 0
    counts = [stop - start for start, stop in spans]
    return pl.pallas_call(
        functools.partial(pack_kernel, 0 if whole else first),
        grid=(1,),
        in_specs=[pl.BlockSpec((block, high, width), lambda i: (at, 0, 0))],
        out_specs=[
            pl.BlockSpec((count, high, per * width), lambda i: (0, 0, 0)) for count in counts
        ],
        out_shape=[
            jax.ShapeDtypeStruct((count, high, per * width), tentative.dtype) for count in counts
        ],
        compiler_params=PARAMS,
        cost_estimate=cost(0, 5 * sum(counts) * per * high * width),
    )(tentative)


def prolong_kernel(first, table, labels, off, diag, inverse, own, near_a, near_b, out, *wides):
    step = near_a.shape[0]
    slots, size = off.shape[1], off.shape[2]
    window = CW * size
    start = 2 * RQ * (first + pl.program_id(0) * step)

    @pl.when(pl.program_id(0) == 0)
    def _():
        for wide in wides:
            wide[3 * RQ] = jnp.zeros((size, window), wide.dtype)

    for c, wide in enumerate(wides):
        m = c // 2
        for k in range(RQ):
            local = RQ * c + k
            j = local % (2 * RQ)
            lanes = slice(j * size, (j + 1) * size)
            for side, block in enumerate((near_a[m, :, lanes], own[local], near_b[m, :, lanes])):
                label = labels[side, start + local]
                for w in range(CW):
                    wide[side * RQ + k, :, w * size : (w + 1) * size] = jnp.where(
                        label == w, block, jnp.zeros_like(block)
                    )
    sums = []
    for c, wide in enumerate(wides):
        for k in range(RQ):
            local = RQ * c + k
            total = jnp.dot(diag[local], wide[RQ + k], preferred_element_type=jnp.float32)
            for s in range(slots):
                total += jnp.dot(
                    off[local, s],
                    wide[table[s, start + local]],
                    preferred_element_type=jnp.float32,
                )
            sums.append(total.astype(out.dtype))
    for c, wide in enumerate(wides):
        for k in range(RQ):
            local = RQ * c + k
            change = jnp.dot(inverse[local], sums[local], preferred_element_type=jnp.float32)
            out[c, :, k * window : (k + 1) * window] = (
                wide[RQ + k].astype(jnp.float32) - OMEGA * change
            ).astype(out.dtype)


def prolong_rows(table, labels, off, diag, inverse, tentative, near_a, near_b, first):
    per = 2 * RQ
    count, high, _ = near_a.shape
    slots, size = off.shape[1], off.shape[2]
    window = CW * size
    step = step_of(first, count)

    def rows(i):
        return (i + first // step, 0, 0)

    square = pl.BlockSpec((per * step, size, size), rows)
    packed = pl.BlockSpec((step, high, per * size), lambda i: (i, 0, 0))
    return pl.pallas_call(
        functools.partial(prolong_kernel, first),
        grid=(count // step,),
        in_specs=[
            SMEM,
            SMEM,
            pl.BlockSpec((per * step, slots, size, size), lambda i: rows(i) + (0,)),
            square,
            square,
            square,
            packed,
            packed,
        ],
        out_specs=pl.BlockSpec((2 * step, size, RQ * window), lambda i: (i, 0, 0)),
        out_shape=jax.ShapeDtypeStruct((2 * count, size, RQ * window), tentative.dtype),
        scratch_shapes=[pltpu.VMEM((3 * RQ + 1, size, window), tentative.dtype)] * (2 * step),
        compiler_params=PARAMS,
        cost_estimate=cost(
            2 * count * per * (slots + 2) * size * size * window,
            2 * count * per * (slots + 7) * size * size,
        ),
    )(table, labels, off, diag, inverse, tentative, near_a, near_b)


def coarse_kernel(first, table, place, off, diag, own, near_a, near_b, keep, send, *scratch):
    step = keep.shape[1]
    slots, size = off.shape[1], off.shape[2]
    window = CW * size
    halves, high = keep.shape[0], keep.shape[2]
    col = place[0]
    start = 2 * RQ * (first + pl.program_id(0) * step)
    fields, stiffs, wholes = (scratch[2 * step * i : 2 * step * (i + 1)] for i in range(3))

    @pl.when(pl.program_id(0) == 0)
    def _():
        for field in fields:
            field[3 * RQ] = jnp.zeros((size, window), field.dtype)

    for c, field in enumerate(fields):
        for k in range(RQ):
            lanes = slice(k * window, (k + 1) * window)
            for side, source in enumerate((near_a, own, near_b)):
                field[side * RQ + k] = source[c, :, lanes]
    for c, (field, stiff) in enumerate(zip(fields, stiffs)):
        for k in range(RQ):
            local = RQ * c + k
            total = jnp.dot(diag[local], field[RQ + k], preferred_element_type=jnp.float32)
            for s in range(slots):
                total += jnp.dot(
                    off[local, s],
                    field[table[s, start + local]],
                    preferred_element_type=jnp.float32,
                )
            stiff[k * size : (k + 1) * size, :] = total.astype(stiff.dtype)
    for field, stiff, whole in zip(fields, stiffs, wholes):
        left = field[RQ : 2 * RQ].reshape(RQ * size, window)
        block = lax.dot_general(
            left, stiff[...], (((0,), (0,)), ((), ())), preferred_element_type=jnp.float32
        )
        for piece in range(2 * halves):
            whole[piece] = block[piece * high : (piece + 1) * high]
    for c, whole in enumerate(wholes):
        lanes = slice(c % 2 * window, (c % 2 + 1) * window)
        for h in range(halves):
            keep[h, c // 2, :, lanes] = whole[col ^ (2 * h)]
            send[h, c // 2, :, lanes] = whole[col ^ (2 * h + 1)].astype(send.dtype)


def coarse_rows(table, place, off, diag, own, near_a, near_b, first, columns):
    per = 2 * RQ
    count = own.shape[0] // 2
    slots, size = off.shape[1], off.shape[2]
    window = CW * size
    halves, high = columns // 2, window // columns
    step = step_of(first, count)

    def rows(i):
        return (i + first // step, 0, 0)

    packed = pl.BlockSpec((2 * step, size, RQ * window), lambda i: (i, 0, 0))
    result = pl.BlockSpec((halves, step, high, 2 * window), lambda i: (0, i, 0, 0))
    shape = (halves, count, high, 2 * window)
    return pl.pallas_call(
        functools.partial(coarse_kernel, first),
        grid=(count // step,),
        in_specs=[
            SMEM,
            SMEM,
            pl.BlockSpec((per * step, slots, size, size), lambda i: rows(i) + (0,)),
            pl.BlockSpec((per * step, size, size), rows),
            packed,
            packed,
            packed,
        ],
        out_specs=[result, result],
        out_shape=[
            jax.ShapeDtypeStruct(shape, jnp.float32),
            jax.ShapeDtypeStruct(shape, own.dtype),
        ],
        scratch_shapes=[pltpu.VMEM((3 * RQ + 1, size, window), own.dtype)] * (2 * step)
        + [pltpu.VMEM((RQ * size, window), own.dtype)] * (2 * step)
        + [pltpu.VMEM((columns, high, window), jnp.float32)] * (2 * step),
        compiler_params=PARAMS,
        cost_estimate=cost(
            2 * count * per * (slots + 3) * size * size * window,
            2 * count * per * (slots + 12) * size * size,
        ),
    )(table, place, off, diag, own, near_a, near_b)


def add_groups(targets, place, sides, first, sums):
    groups = sums.shape[0] - 1
    window = sums.shape[2]
    row = place[1]
    for side, source in enumerate(sides):

        def one(m, source=source, side=side):
            for u in range(2):
                target = targets[side, 2 * (first + m) + u]
                away = (target // G_DEV) ^ row
                spot = jnp.where(away % 2 == 0, away // 2 * G_DEV + target % G_DEV, groups)
                sums[spot] += source[m, :, u * window : (u + 1) * window].astype(jnp.float32)

        for m in range(source.shape[0]):
            one(m)


def bring(sources, buffers, sems):
    copies = [
        pltpu.make_async_copy(source, buffer, sems.at[i])
        for i, (source, buffer) in enumerate(zip(sources, buffers))
    ]
    for copy in copies:
        copy.start()
    return copies


def gather_kernel(starts, targets, place, *refs):
    count = 2 * len(starts)
    sources, sums, buffers, sems = refs[:count], refs[count], refs[count + 1 : -1], refs[-1]
    copies = bring(sources, buffers, sems)
    sums[...] = jnp.zeros_like(sums)
    for part, first in enumerate(starts):
        for copy in copies[2 * part : 2 * part + 2]:
            copy.wait()
        add_groups(targets, place, buffers[2 * part : 2 * part + 2], first, sums)


def gather_groups(targets, place, parts, starts, rows):
    _, high, lanes = parts[0][0].shape
    shape = (rows // 2 * G_DEV + 1, high, lanes // 2)
    flat = [array for pair in parts for array in pair]
    total = sum(array.size for array in flat)
    return pl.pallas_call(
        functools.partial(gather_kernel, starts),
        in_specs=[SMEM, SMEM] + [ANY] * len(flat),
        out_specs=VMEM,
        out_shape=jax.ShapeDtypeStruct(shape, jnp.float32),
        scratch_shapes=[pltpu.VMEM(array.shape, array.dtype) for array in flat]
        + [pltpu.SemaphoreType.DMA((len(flat),))],
        compiler_params=SMALL,
        cost_estimate=cost(total, 4 * total),
    )(targets, place, *flat)


def split_kernel(first, targets, place, early, mine, theirs, keep, odd, even, sums, *scratch):
    buffers, sems = scratch[:-1], scratch[-1]
    for copy in bring((early, mine, theirs), (sums,) + buffers, sems):
        copy.wait()
    add_groups(targets, place, buffers, first, sums)
    window = sums.shape[2]
    for h in range(keep.shape[0]):
        send = odd if h % 2 else even
        for p in range(keep.shape[1]):
            for u in range(2):
                lanes = slice(u * window, (u + 1) * window)
                inner = 2 * p + u
                keep[h, p, :, lanes] = sums[2 * h * G_DEV + inner]
                send[h // 2, p, :, lanes] = sums[(2 * h + 1) * G_DEV + inner].astype(send.dtype)


def split_groups(targets, place, early, mine, theirs, first, rows):
    _, high, lanes = mine.shape
    shape = (rows // 4, G_DEV // 2, high, lanes)
    half = jax.ShapeDtypeStruct((rows // 8,) + shape[1:], mine.dtype)
    return pl.pallas_call(
        functools.partial(split_kernel, first),
        in_specs=[SMEM, SMEM, ANY, ANY, ANY],
        out_specs=[VMEM, VMEM, VMEM],
        out_shape=[jax.ShapeDtypeStruct(shape, jnp.float32), half, half],
        scratch_shapes=[
            pltpu.VMEM(early.shape, jnp.float32),
            pltpu.VMEM(mine.shape, mine.dtype),
            pltpu.VMEM(theirs.shape, theirs.dtype),
            pltpu.SemaphoreType.DMA((3,)),
        ],
        compiler_params=SMALL,
        cost_estimate=cost(early.size, 10 * early.size),
    )(targets, place, early, mine, theirs)


def finish_kernel(keep_ref, *refs):
    others, out_ref = refs[:-1], refs[-1]
    window = out_ref.shape[2]
    for p in range(keep_ref.shape[1]):
        total = keep_ref[0, p]
        for other in others:
            total += other[0, p].astype(jnp.float32)
        for u in range(2):
            out_ref[2 * p + u] = total[:, u * window : (u + 1) * window]


def finish(keep, *others):
    _, pairs, high, lanes = keep.shape
    block = pl.BlockSpec((1, pairs, high, lanes), lambda i: (0, 0, 0, 0))
    return pl.pallas_call(
        finish_kernel,
        grid=(1,),
        in_specs=[block] * (1 + len(others)),
        out_specs=pl.BlockSpec((2 * pairs, high, lanes // 2), lambda i: (0, 0, 0)),
        out_shape=jax.ShapeDtypeStruct((2 * pairs, high, lanes // 2), jnp.float32),
        compiler_params=PARAMS,
        cost_estimate=cost(pairs * high * lanes, 10 * pairs * high * lanes),
    )(keep, *others)


def flip(count, bit):
    return [(i, i ^ bit) for i in range(count)]


def exchange(keep, send, axis, count, bit, link):
    terms = [(keep, 1)]
    while True:
        route = flip(count, bit)
        if isinstance(send, tuple):
            odd = lax.ppermute(send[0], axis, route)
            arrived = (lax.ppermute(send[1], axis, route), 1)
        else:
            arrived = (lax.ppermute(send, axis, route), 2)
            odd = arrived[0][1::2]
        bit *= 2
        if bit == count:
            return [term for term, _ in terms] + [arrived[0]]
        leave = sum(term[stride :: 2 * stride].astype(jnp.float32) for term, stride in terms)
        send = (leave + odd.astype(jnp.float32)).astype(link)
        terms = [(term, 2 * stride) for term, stride in terms] + [arrived]


def on_device(
    off_blocks,
    neighbour,
    active,
    diag_blocks,
    diag_inverse,
    tentative,
    aggregate,
    owner_row,
    owner_group,
):
    columns, rows = lax.axis_size("col"), lax.axis_size("row")
    col, row = lax.axis_index("col"), lax.axis_index("row")
    assert columns & (columns - 1) == 0 and columns >= 2
    assert rows & (rows - 1) == 0 and rows >= 8
    link = tentative.dtype
    groups = tentative.shape[0] // (2 * RQ)

    pair_a = flip(columns, 1)
    pair_b = [(i, (i + 1) % columns if i % 2 else (i - 1) % columns) for i in range(columns)]

    bounds = [groups * edge // EDGES[-1] for edge in EDGES]
    spans = list(zip(bounds[:-1], bounds[1:]))

    def both(block):
        near_b = lax.ppermute(block, "col", pair_b)
        near_a = lax.ppermute(block, "col", pair_a)
        return near_a, near_b

    packed = list(pack_rows(tentative, spans[:1]))
    packed += pack_rows(tentative, spans[1:])
    halos = [both(block) for block in packed]
    label_a, label_b = both(aggregate)
    labels = jnp.stack([label_a, aggregate, label_b])
    targets = owner_row[:, 0] * G_DEV + owner_group
    other_targets = lax.ppermute(targets, "row", flip(rows, 1))
    targets = jnp.stack([targets, other_targets])
    side = neighbour // RQ
    side = jnp.where(col % 2 == 0, 2 - side, side)
    table = jnp.where(active != 0, side * RQ + neighbour % RQ, 3 * RQ).T
    place = jnp.stack([col, row])
    labels, targets, table, place = lax.optimization_barrier((labels, targets, table, place))

    fields = []
    for (low, high), (near_a, near_b) in zip(spans, halos):
        field = prolong_rows(
            table, labels, off_blocks, diag_blocks, diag_inverse, tentative, near_a, near_b, low
        )
        fields.append((field, *both(field)))
    parts = []
    for (low, high), (field, near_a, near_b) in zip(spans, fields):
        keep, send = coarse_rows(
            table, place, off_blocks, diag_blocks, field, near_a, near_b, low, columns
        )
        terms = exchange(keep, send, "col", columns, 1, link)
        total = sum(term[0].astype(jnp.float32) for term in terms).astype(link)
        other = lax.ppermute(total, "row", flip(rows, 1))
        parts.append((total, other))
    early = gather_groups(targets, place, parts[:-1], [low for low, _ in spans[:-1]], rows)
    keep, *send = split_groups(targets, place, early, *parts[-1], spans[-1][0], rows)
    return finish(*exchange(keep, tuple(send), "row", rows, 2, link))


def solution(mesh):
    return jax.shard_map(
        on_device,
        mesh=mesh,
        in_specs=(
            P(("row", "col"), None, None, None),
            P(("row", "col"), None),
            P(("row", "col"), None),
            P(("row", "col"), None, None),
            P(("row", "col"), None, None),
            P(("row", "col"), None, None),
            P(("row", "col")),
            P("row", None),
            P("row"),
        ),
        out_specs=P("row", "col", None),
        check_vma=False,
    )
```

```python
import functools

import jax
import jax.numpy as jnp
from jax import lax
from jax.experimental import pallas as pl
from jax.experimental.pallas import tpu as pltpu
from jax.sharding import PartitionSpec as P


CW = 2
RQ = 2
G_DEV = 8
OMEGA = 0.6

EDGES = (0, 6, 10, 14, 16)
STEP = 2


VMEM = pl.BlockSpec(memory_space=pltpu.VMEM)
SMEM = pl.BlockSpec(memory_space=pltpu.SMEM)
ANY = pl.BlockSpec(memory_space=pl.ANY)
PARAMS = pltpu.CompilerParams(vmem_limit_bytes=25165824)
ALONE = pltpu.CompilerParams(vmem_limit_bytes=67043328)


def step_of(first, count):
    return STEP if count % STEP == 0 and first % STEP == 0 else 1


def cost(flops, moved):
    return pl.CostEstimate(flops=int(flops), bytes_accessed=int(moved), transcendentals=0)


def pack_kernel(first, rows_ref, *outs):
    per = 2 * RQ
    width = rows_ref.shape[2]
    base = per * first
    for out in outs:
        for m in range(out.shape[0]):
            for j in range(per):
                out[m, :, j * width : (j + 1) * width] = rows_ref[base + per * m + j]
        base += per * out.shape[0]


def pack_rows(tentative, spans):
    per = 2 * RQ
    _, high, width = tentative.shape
    first, last = spans[0][0], spans[-1][1]
    whole = first % (last - first) == 0
    block = per * (last - first if whole else last)
    at = first // (last - first) if whole else 0
    counts = [stop - start for start, stop in spans]
    return pl.pallas_call(
        functools.partial(pack_kernel, 0 if whole else first),
        grid=(1,),
        in_specs=[pl.BlockSpec((block, high, width), lambda i: (at, 0, 0))],
        out_specs=[
            pl.BlockSpec((count, high, per * width), lambda i: (0, 0, 0)) for count in counts
        ],
        out_shape=[
            jax.ShapeDtypeStruct((count, high, per * width), tentative.dtype) for count in counts
        ],
        compiler_params=PARAMS if first else ALONE,
        cost_estimate=cost(0, 5 * sum(counts) * per * high * width),
    )(tentative)


def prolong_kernel(first, table, labels, off, diag, inverse, own, near_a, near_b, out, *wides):
    step = len(wides) // 2
    slots, size = off.shape[1], off.shape[2]
    window = CW * size
    base = pl.program_id(0) * step
    start = 2 * RQ * (first + base)

    @pl.when(pl.program_id(0) == 0)
    def _():
        for wide in wides:
            wide[3 * RQ] = jnp.zeros((size, window), wide.dtype)

    for c, wide in enumerate(wides):
        m = c // 2
        for k in range(RQ):
            local = RQ * c + k
            j = local % (2 * RQ)
            lanes = slice(j * size, (j + 1) * size)
            for side, block in enumerate(
                (near_a[base + m, :, lanes], own[local], near_b[base + m, :, lanes])
            ):
                label = labels[side, start + local]
                for w in range(CW):
                    wide[side * RQ + k, :, w * size : (w + 1) * size] = jnp.where(
                        label == w, block, jnp.zeros_like(block)
                    )
    sums = []
    for c, wide in enumerate(wides):
        for k in range(RQ):
            local = RQ * c + k
            total = jnp.dot(diag[local], wide[RQ + k], preferred_element_type=jnp.float32)
            for s in range(slots):
                total += jnp.dot(
                    off[local, s],
                    wide[table[s, start + local]],
                    preferred_element_type=jnp.float32,
                )
            sums.append(total.astype(out.dtype))
    for c, wide in enumerate(wides):
        for k in range(RQ):
            local = RQ * c + k
            change = jnp.dot(inverse[local], sums[local], preferred_element_type=jnp.float32)
            out[2 * base + c, :, k * window : (k + 1) * window] = (
                wide[RQ + k].astype(jnp.float32) - OMEGA * change
            ).astype(out.dtype)


def prolong_rows(table, labels, off, diag, inverse, tentative, near_a, near_b, first):
    per = 2 * RQ
    count = near_a.shape[0]
    slots, size = off.shape[1], off.shape[2]
    window = CW * size
    step = step_of(first, count)

    def rows(i):
        return (i + first // step, 0, 0)

    square = pl.BlockSpec((per * step, size, size), rows)
    return pl.pallas_call(
        functools.partial(prolong_kernel, first),
        grid=(count // step,),
        in_specs=[
            SMEM,
            SMEM,
            pl.BlockSpec((per * step, slots, size, size), lambda i: rows(i) + (0,)),
            square,
            square,
            square,
            VMEM,
            VMEM,
        ],
        out_specs=VMEM,
        out_shape=jax.ShapeDtypeStruct((2 * count, size, RQ * window), tentative.dtype),
        scratch_shapes=[pltpu.VMEM((3 * RQ + 1, size, window), tentative.dtype)] * (2 * step),
        compiler_params=PARAMS,
        cost_estimate=cost(
            2 * count * per * (slots + 2) * size * size * window,
            2 * count * per * (slots + 7) * size * size,
        ),
    )(table, labels, off, diag, inverse, tentative, near_a, near_b)


def coarse_kernel(first, table, place, off, diag, own, near_a, near_b, keep, send, *scratch):
    step = len(scratch) // 6
    slots, size = off.shape[1], off.shape[2]
    window = CW * size
    halves, high = keep.shape[0], keep.shape[2]
    col = place[0]
    base = pl.program_id(0) * step
    start = 2 * RQ * (first + base)
    fields, stiffs, wholes = (scratch[2 * step * i : 2 * step * (i + 1)] for i in range(3))

    @pl.when(pl.program_id(0) == 0)
    def _():
        for field in fields:
            field[3 * RQ] = jnp.zeros((size, window), field.dtype)

    for c, field in enumerate(fields):
        for k in range(RQ):
            lanes = slice(k * window, (k + 1) * window)
            for side, source in enumerate((near_a, own, near_b)):
                field[side * RQ + k] = source[2 * base + c, :, lanes]
    for c, (field, stiff) in enumerate(zip(fields, stiffs)):
        for k in range(RQ):
            local = RQ * c + k
            total = jnp.dot(diag[local], field[RQ + k], preferred_element_type=jnp.float32)
            for s in range(slots):
                total += jnp.dot(
                    off[local, s],
                    field[table[s, start + local]],
                    preferred_element_type=jnp.float32,
                )
            stiff[k * size : (k + 1) * size, :] = total.astype(stiff.dtype)
    for field, stiff, whole in zip(fields, stiffs, wholes):
        left = field[RQ : 2 * RQ].reshape(RQ * size, window)
        block = lax.dot_general(
            left, stiff[...], (((0,), (0,)), ((), ())), preferred_element_type=jnp.float32
        )
        for piece in range(2 * halves):
            whole[piece] = block[piece * high : (piece + 1) * high]
    for c, whole in enumerate(wholes):
        lanes = slice(c % 2 * window, (c % 2 + 1) * window)
        for h in range(halves):
            keep[h, base + c // 2, :, lanes] = whole[col ^ (2 * h)]
            send[h, base + c // 2, :, lanes] = whole[col ^ (2 * h + 1)].astype(send.dtype)


def coarse_rows(table, place, off, diag, own, near_a, near_b, first, columns):
    per = 2 * RQ
    count = own.shape[0] // 2
    slots, size = off.shape[1], off.shape[2]
    window = CW * size
    halves, high = columns // 2, window // columns
    step = step_of(first, count)

    def rows(i):
        return (i + first // step, 0, 0)

    shape = (halves, count, high, 2 * window)
    return pl.pallas_call(
        functools.partial(coarse_kernel, first),
        grid=(count // step,),
        in_specs=[
            SMEM,
            SMEM,
            pl.BlockSpec((per * step, slots, size, size), lambda i: rows(i) + (0,)),
            pl.BlockSpec((per * step, size, size), rows),
            VMEM,
            VMEM,
            VMEM,
        ],
        out_specs=[VMEM, VMEM],
        out_shape=[
            jax.ShapeDtypeStruct(shape, jnp.float32),
            jax.ShapeDtypeStruct(shape, own.dtype),
        ],
        scratch_shapes=[pltpu.VMEM((3 * RQ + 1, size, window), own.dtype)] * (2 * step)
        + [pltpu.VMEM((RQ * size, window), own.dtype)] * (2 * step)
        + [pltpu.VMEM((columns, high, window), jnp.float32)] * (2 * step),
        compiler_params=PARAMS,
        cost_estimate=cost(
            2 * count * per * (slots + 3) * size * size * window,
            2 * count * per * (slots + 12) * size * size,
        ),
    )(table, place, off, diag, own, near_a, near_b)


def add_groups(targets, place, sides, first, sums):
    groups = sums.shape[0] - 1
    window = sums.shape[2]
    row = place[1]
    for side, source in enumerate(sides):

        def one(m, source=source, side=side):
            for u in range(2):
                target = targets[side, 2 * (first + m) + u]
                away = (target // G_DEV) ^ row
                spot = jnp.where(away % 2 == 0, away // 2 * G_DEV + target % G_DEV, groups)
                sums[spot] += source[m, :, u * window : (u + 1) * window].astype(jnp.float32)

        for m in range(source.shape[0]):
            one(m)


def bring(sources, buffers, sems):
    copies = [
        pltpu.make_async_copy(source, buffer, sems.at[i])
        for i, (source, buffer) in enumerate(zip(sources, buffers))
    ]
    for copy in copies:
        copy.start()
    return copies


def gather_kernel(starts, targets, place, *refs):
    count = 2 * len(starts)
    sources, sums, buffers, sems = refs[:count], refs[count], refs[count + 1 : -1], refs[-1]
    copies = bring(sources, buffers, sems)
    sums[...] = jnp.zeros_like(sums)
    for part, first in enumerate(starts):
        for copy in copies[2 * part : 2 * part + 2]:
            copy.wait()
        add_groups(targets, place, buffers[2 * part : 2 * part + 2], first, sums)


def gather_groups(targets, place, parts, starts, rows):
    _, high, lanes = parts[0][0].shape
    shape = (rows // 2 * G_DEV + 1, high, lanes // 2)
    flat = [array for pair in parts for array in pair]
    total = sum(array.size for array in flat)
    return pl.pallas_call(
        functools.partial(gather_kernel, starts),
        in_specs=[SMEM, SMEM] + [ANY] * len(flat),
        out_specs=VMEM,
        out_shape=jax.ShapeDtypeStruct(shape, jnp.float32),
        scratch_shapes=[pltpu.VMEM(array.shape, array.dtype) for array in flat]
        + [pltpu.SemaphoreType.DMA((len(flat),))],
        compiler_params=PARAMS,
        cost_estimate=cost(total, 4 * total),
    )(targets, place, *flat)


def split_kernel(first, targets, place, early, mine, theirs, keep, odd, even, sums, *scratch):
    buffers, sems = scratch[:-1], scratch[-1]
    for copy in bring((early, mine, theirs), (sums,) + buffers, sems):
        copy.wait()
    add_groups(targets, place, buffers, first, sums)
    window = sums.shape[2]
    for h in range(keep.shape[0]):
        send = odd if h % 2 else even
        for p in range(keep.shape[1]):
            for u in range(2):
                lanes = slice(u * window, (u + 1) * window)
                inner = 2 * p + u
                keep[h, p, :, lanes] = sums[2 * h * G_DEV + inner]
                send[h // 2, p, :, lanes] = sums[(2 * h + 1) * G_DEV + inner].astype(send.dtype)


def split_groups(targets, place, early, mine, theirs, first, rows):
    _, high, lanes = mine.shape
    shape = (rows // 4, G_DEV // 2, high, lanes)
    half = jax.ShapeDtypeStruct((rows // 8,) + shape[1:], mine.dtype)
    return pl.pallas_call(
        functools.partial(split_kernel, first),
        in_specs=[SMEM, SMEM, ANY, ANY, ANY],
        out_specs=[VMEM, VMEM, VMEM],
        out_shape=[jax.ShapeDtypeStruct(shape, jnp.float32), half, half],
        scratch_shapes=[
            pltpu.VMEM(early.shape, jnp.float32),
            pltpu.VMEM(mine.shape, mine.dtype),
            pltpu.VMEM(theirs.shape, theirs.dtype),
            pltpu.SemaphoreType.DMA((3,)),
        ],
        compiler_params=PARAMS,
        cost_estimate=cost(early.size, 10 * early.size),
    )(targets, place, early, mine, theirs)


def finish_kernel(keep_ref, *refs):
    others, out_ref = refs[:-1], refs[-1]
    window = out_ref.shape[2]
    for p in range(keep_ref.shape[1]):
        total = keep_ref[0, p]
        for other in others:
            total += other[0, p].astype(jnp.float32)
        for u in range(2):
            out_ref[2 * p + u] = total[:, u * window : (u + 1) * window]


def finish(keep, *others):
    _, pairs, high, lanes = keep.shape
    return pl.pallas_call(
        finish_kernel,
        in_specs=[VMEM] * (1 + len(others)),
        out_specs=VMEM,
        out_shape=jax.ShapeDtypeStruct((2 * pairs, high, lanes // 2), jnp.float32),
        compiler_params=PARAMS,
        cost_estimate=cost(pairs * high * lanes, 10 * pairs * high * lanes),
    )(keep, *others)


def flip(count, bit):
    return [(i, i ^ bit) for i in range(count)]


def exchange(keep, send, axis, count, bit, link):
    terms = [(keep, 1)]
    while True:
        route = flip(count, bit)
        if isinstance(send, tuple):
            odd = lax.ppermute(send[0], axis, route)
            arrived = (lax.ppermute(send[1], axis, route), 1)
        else:
            arrived = (lax.ppermute(send, axis, route), 2)
            odd = arrived[0][1::2]
        bit *= 2
        if bit == count:
            return [term for term, _ in terms] + [arrived[0]]
        leave = sum(term[stride :: 2 * stride].astype(jnp.float32) for term, stride in terms)
        send = (leave + odd.astype(jnp.float32)).astype(link)
        terms = [(term, 2 * stride) for term, stride in terms] + [arrived]


def on_device(
    off_blocks,
    neighbour,
    active,
    diag_blocks,
    diag_inverse,
    tentative,
    aggregate,
    owner_row,
    owner_group,
):
    columns, rows = lax.axis_size("col"), lax.axis_size("row")
    col, row = lax.axis_index("col"), lax.axis_index("row")
    assert columns & (columns - 1) == 0 and columns >= 2
    assert rows & (rows - 1) == 0 and rows >= 8
    link = tentative.dtype
    groups = tentative.shape[0] // (2 * RQ)

    pair_a = flip(columns, 1)
    pair_b = [(i, (i + 1) % columns if i % 2 else (i - 1) % columns) for i in range(columns)]

    bounds = [groups * edge // EDGES[-1] for edge in EDGES]
    spans = list(zip(bounds[:-1], bounds[1:]))

    def both(block):
        near_b = lax.ppermute(block, "col", pair_b)
        near_a = lax.ppermute(block, "col", pair_a)
        return near_a, near_b

    packed = list(pack_rows(tentative, spans[:1]))
    packed += pack_rows(tentative, spans[1:])
    halos = [both(block) for block in packed]
    label_a, label_b = both(aggregate)
    labels = jnp.stack([label_a, aggregate, label_b])
    targets = owner_row[:, 0] * G_DEV + owner_group
    other_targets = lax.ppermute(targets, "row", flip(rows, 1))
    targets = jnp.stack([targets, other_targets])
    side = neighbour // RQ
    side = jnp.where(col % 2 == 0, 2 - side, side)
    table = jnp.where(active != 0, side * RQ + neighbour % RQ, 3 * RQ).T
    place = jnp.stack([col, row])
    labels, targets, table, place = lax.optimization_barrier((labels, targets, table, place))

    fields = []
    for (low, high), (near_a, near_b) in zip(spans, halos):
        field = prolong_rows(
            table, labels, off_blocks, diag_blocks, diag_inverse, tentative, near_a, near_b, low
        )
        fields.append((field, *both(field)))
    parts = []
    for (low, high), (field, near_a, near_b) in zip(spans, fields):
        keep, send = coarse_rows(
            table, place, off_blocks, diag_blocks, field, near_a, near_b, low, columns
        )
        terms = exchange(keep, send, "col", columns, 1, link)
        total = sum(term[0].astype(jnp.float32) for term in terms).astype(link)
        other = lax.ppermute(total, "row", flip(rows, 1))
        parts.append((total, other))
    early = gather_groups(targets, place, parts[:-1], [low for low, _ in spans[:-1]], rows)
    keep, *send = split_groups(targets, place, early, *parts[-1], spans[-1][0], rows)
    return finish(*exchange(keep, tuple(send), "row", rows, 2, link))


def solution(mesh):
    return jax.shard_map(
        on_device,
        mesh=mesh,
        in_specs=(
            P(("row", "col"), None, None, None),
            P(("row", "col"), None),
            P(("row", "col"), None),
            P(("row", "col"), None, None),
            P(("row", "col"), None, None),
            P(("row", "col"), None, None),
            P(("row", "col")),
            P("row", None),
            P("row"),
        ),
        out_specs=P("row", "col", None),
        check_vma=False,
    )
```

```python
import functools

import jax
import jax.numpy as jnp
from jax import lax
from jax.experimental import pallas as pl
from jax.experimental.pallas import tpu as pltpu
from jax.sharding import PartitionSpec as P


CW = 2
RQ = 2
G_DEV = 8
OMEGA = 0.6

EDGES = (0, 6, 10, 14, 16)
STEP = 2


VMEM = pl.BlockSpec(memory_space=pltpu.VMEM)
SMEM = pl.BlockSpec(memory_space=pltpu.SMEM)
ANY = pl.BlockSpec(memory_space=pl.ANY)
PARAMS = pltpu.CompilerParams(vmem_limit_bytes=25165824)
WIDE = pltpu.CompilerParams(vmem_limit_bytes=60817408)
ALONE = pltpu.CompilerParams(vmem_limit_bytes=67043328)


def step_of(first, count):
    return STEP if count % STEP == 0 and first % STEP == 0 else 1


def cost(flops, moved):
    return pl.CostEstimate(flops=int(flops), bytes_accessed=int(moved), transcendentals=0)


def pack_kernel(first, rows_ref, *outs):
    per = 2 * RQ
    width = rows_ref.shape[2]
    base = per * first
    for out in outs:
        for m in range(out.shape[0]):
            for j in range(per):
                out[m, :, j * width : (j + 1) * width] = rows_ref[base + per * m + j]
        base += per * out.shape[0]


def pack_rows(tentative, spans):
    per = 2 * RQ
    _, high, width = tentative.shape
    first, last = spans[0][0], spans[-1][1]
    whole = first % (last - first) == 0
    block = per * (last - first if whole else last)
    at = first // (last - first) if whole else 0
    counts = [stop - start for start, stop in spans]
    return pl.pallas_call(
        functools.partial(pack_kernel, 0 if whole else first),
        grid=(1,),
        in_specs=[pl.BlockSpec((block, high, width), lambda i: (at, 0, 0))],
        out_specs=[
            pl.BlockSpec((count, high, per * width), lambda i: (0, 0, 0)) for count in counts
        ],
        out_shape=[
            jax.ShapeDtypeStruct((count, high, per * width), tentative.dtype) for count in counts
        ],
        compiler_params=PARAMS if first else ALONE,
        cost_estimate=cost(0, 5 * sum(counts) * per * high * width),
    )(tentative)


def prolong_kernel(first, table, labels, off, diag, inverse, own, near_a, near_b, out, *wides):
    step = len(wides) // 2
    slots, size = off.shape[1], off.shape[2]
    window = CW * size
    base = pl.program_id(0) * step
    start = 2 * RQ * (first + base)

    @pl.when(pl.program_id(0) == 0)
    def _():
        for wide in wides:
            wide[3 * RQ] = jnp.zeros((size, window), wide.dtype)

    for c, wide in enumerate(wides):
        m = c // 2
        for k in range(RQ):
            local = RQ * c + k
            j = local % (2 * RQ)
            lanes = slice(j * size, (j + 1) * size)
            for side, block in enumerate(
                (near_a[base + m, :, lanes], own[local], near_b[base + m, :, lanes])
            ):
                label = labels[side, start + local]
                for w in range(CW):
                    wide[side * RQ + k, :, w * size : (w + 1) * size] = jnp.where(
                        label == w, block, jnp.zeros_like(block)
                    )
    sums = []
    for c, wide in enumerate(wides):
        for k in range(RQ):
            local = RQ * c + k
            total = jnp.dot(diag[local], wide[RQ + k], preferred_element_type=jnp.float32)
            for s in range(slots):
                total += jnp.dot(
                    off[local, s],
                    wide[table[s, start + local]],
                    preferred_element_type=jnp.float32,
                )
            sums.append(total.astype(out.dtype))
    for c, wide in enumerate(wides):
        for k in range(RQ):
            local = RQ * c + k
            change = jnp.dot(inverse[local], sums[local], preferred_element_type=jnp.float32)
            out[2 * base + c, :, k * window : (k + 1) * window] = (
                wide[RQ + k].astype(jnp.float32) - OMEGA * change
            ).astype(out.dtype)


def prolong_rows(table, labels, off, diag, inverse, tentative, near_a, near_b, first):
    per = 2 * RQ
    count = near_a.shape[0]
    slots, size = off.shape[1], off.shape[2]
    window = CW * size
    step = step_of(first, count)

    def rows(i):
        return (i + first // step, 0, 0)

    square = pl.BlockSpec((per * step, size, size), rows)
    return pl.pallas_call(
        functools.partial(prolong_kernel, first),
        grid=(count // step,),
        in_specs=[
            SMEM,
            SMEM,
            pl.BlockSpec((per * step, slots, size, size), lambda i: rows(i) + (0,)),
            square,
            square,
            square,
            VMEM,
            VMEM,
        ],
        out_specs=VMEM,
        out_shape=jax.ShapeDtypeStruct((2 * count, size, RQ * window), tentative.dtype),
        scratch_shapes=[pltpu.VMEM((3 * RQ + 1, size, window), tentative.dtype)] * (2 * step),
        compiler_params=PARAMS if first else WIDE,
        cost_estimate=cost(
            2 * count * per * (slots + 2) * size * size * window,
            2 * count * per * (slots + 7) * size * size,
        ),
    )(table, labels, off, diag, inverse, tentative, near_a, near_b)


def coarse_kernel(first, table, place, off, diag, own, near_a, near_b, keep, send, *scratch):
    step = len(scratch) // 6
    slots, size = off.shape[1], off.shape[2]
    window = CW * size
    halves, high = keep.shape[0], keep.shape[2]
    col = place[0]
    base = pl.program_id(0) * step
    start = 2 * RQ * (first + base)
    fields, stiffs, wholes = (scratch[2 * step * i : 2 * step * (i + 1)] for i in range(3))

    @pl.when(pl.program_id(0) == 0)
    def _():
        for field in fields:
            field[3 * RQ] = jnp.zeros((size, window), field.dtype)

    for c, field in enumerate(fields):
        for k in range(RQ):
            lanes = slice(k * window, (k + 1) * window)
            for side, source in enumerate((near_a, own, near_b)):
                field[side * RQ + k] = source[2 * base + c, :, lanes]
    for c, (field, stiff) in enumerate(zip(fields, stiffs)):
        for k in range(RQ):
            local = RQ * c + k
            total = jnp.dot(diag[local], field[RQ + k], preferred_element_type=jnp.float32)
            for s in range(slots):
                total += jnp.dot(
                    off[local, s],
                    field[table[s, start + local]],
                    preferred_element_type=jnp.float32,
                )
            stiff[k * size : (k + 1) * size, :] = total.astype(stiff.dtype)
    for field, stiff, whole in zip(fields, stiffs, wholes):
        left = field[RQ : 2 * RQ].reshape(RQ * size, window)
        block = lax.dot_general(
            left, stiff[...], (((0,), (0,)), ((), ())), preferred_element_type=jnp.float32
        )
        for piece in range(2 * halves):
            whole[piece] = block[piece * high : (piece + 1) * high]
    for c, whole in enumerate(wholes):
        lanes = slice(c % 2 * window, (c % 2 + 1) * window)
        for h in range(halves):
            keep[h, base + c // 2, :, lanes] = whole[col ^ (2 * h)]
            send[h, base + c // 2, :, lanes] = whole[col ^ (2 * h + 1)].astype(send.dtype)


def coarse_rows(table, place, off, diag, own, near_a, near_b, first, columns):
    per = 2 * RQ
    count = own.shape[0] // 2
    slots, size = off.shape[1], off.shape[2]
    window = CW * size
    halves, high = columns // 2, window // columns
    step = step_of(first, count)

    def rows(i):
        return (i + first // step, 0, 0)

    shape = (halves, count, high, 2 * window)
    return pl.pallas_call(
        functools.partial(coarse_kernel, first),
        grid=(count // step,),
        in_specs=[
            SMEM,
            SMEM,
            pl.BlockSpec((per * step, slots, size, size), lambda i: rows(i) + (0,)),
            pl.BlockSpec((per * step, size, size), rows),
            VMEM,
            VMEM,
            VMEM,
        ],
        out_specs=[VMEM, VMEM],
        out_shape=[
            jax.ShapeDtypeStruct(shape, jnp.float32),
            jax.ShapeDtypeStruct(shape, own.dtype),
        ],
        scratch_shapes=[pltpu.VMEM((3 * RQ + 1, size, window), own.dtype)] * (2 * step)
        + [pltpu.VMEM((RQ * size, window), own.dtype)] * (2 * step)
        + [pltpu.VMEM((columns, high, window), jnp.float32)] * (2 * step),
        compiler_params=PARAMS,
        cost_estimate=cost(
            2 * count * per * (slots + 3) * size * size * window,
            2 * count * per * (slots + 12) * size * size,
        ),
    )(table, place, off, diag, own, near_a, near_b)


def add_groups(targets, place, sides, first, sums):
    groups = sums.shape[0] - 1
    window = sums.shape[2]
    row = place[1]
    for side, source in enumerate(sides):

        def one(m, source=source, side=side):
            for u in range(2):
                target = targets[side, 2 * (first + m) + u]
                away = (target // G_DEV) ^ row
                spot = jnp.where(away % 2 == 0, away // 2 * G_DEV + target % G_DEV, groups)
                sums[spot] += source[m, :, u * window : (u + 1) * window].astype(jnp.float32)

        for m in range(source.shape[0]):
            one(m)


def bring(sources, buffers, sems):
    copies = [
        pltpu.make_async_copy(source, buffer, sems.at[i])
        for i, (source, buffer) in enumerate(zip(sources, buffers))
    ]
    for copy in copies:
        copy.start()
    return copies


def gather_kernel(starts, targets, place, *refs):
    count = 2 * len(starts)
    sources, sums, buffers, sems = refs[:count], refs[count], refs[count + 1 : -1], refs[-1]
    copies = bring(sources, buffers, sems)
    sums[...] = jnp.zeros_like(sums)
    for part, first in enumerate(starts):
        for copy in copies[2 * part : 2 * part + 2]:
            copy.wait()
        sides = [buffer.at[0] for buffer in buffers[2 * part : 2 * part + 2]]
        add_groups(targets, place, sides, first, sums)


def gather_groups(targets, place, parts, starts, rows):
    _, _, high, lanes = parts[0][0].shape
    shape = (rows // 2 * G_DEV + 1, high, lanes // 2)
    flat = [array for pair in parts for array in pair]
    total = sum(array.size for array in flat)
    return pl.pallas_call(
        functools.partial(gather_kernel, starts),
        in_specs=[SMEM, SMEM] + [ANY] * len(flat),
        out_specs=VMEM,
        out_shape=jax.ShapeDtypeStruct(shape, jnp.float32),
        scratch_shapes=[pltpu.VMEM(array.shape, array.dtype) for array in flat]
        + [pltpu.SemaphoreType.DMA((len(flat),))],
        compiler_params=PARAMS,
        cost_estimate=cost(total, 4 * total),
    )(targets, place, *flat)


def split_kernel(starts, begun, targets, place, *refs):
    count = 2 * len(starts)
    sources, (keep, odd, even, sums) = refs[: begun + count], refs[begun + count :][:4]
    buffers, sems = refs[begun + count + 4 : -1], refs[-1]
    copies = bring(sources, ((sums,) if begun else ()) + buffers, sems)
    window = sums.shape[2]
    for y in range(keep.shape[1]):
        if not begun:
            sums[...] = jnp.zeros_like(sums)
        if y == 0:
            for copy in copies:
                copy.wait()
        for part, first in enumerate(starts):
            sides = [buffer.at[y] for buffer in buffers[2 * part : 2 * part + 2]]
            add_groups(targets, place, sides, first, sums)
        for h in range(keep.shape[0]):
            send = odd if h % 2 else even
            for p in range(keep.shape[2]):
                for u in range(2):
                    lanes = slice(u * window, (u + 1) * window)
                    inner = 2 * p + u
                    keep[h, y, p, :, lanes] = sums[2 * h * G_DEV + inner]
                    away = sums[(2 * h + 1) * G_DEV + inner]
                    send[h // 2, y, p, :, lanes] = away.astype(send.dtype)


def split_groups(targets, place, early, parts, starts, rows):
    layers, _, high, lanes = parts[0][0].shape
    shape = (rows // 4, layers, G_DEV // 2, high, lanes)
    flat = [array for pair in parts for array in pair]
    half = jax.ShapeDtypeStruct((rows // 8,) + shape[1:], flat[0].dtype)
    sums = pltpu.VMEM((rows // 2 * G_DEV + 1, high, lanes // 2), jnp.float32)
    begun = [] if early is None else [early]
    assert layers == 1 or not begun
    return pl.pallas_call(
        functools.partial(split_kernel, starts, len(begun)),
        in_specs=[SMEM, SMEM] + [ANY] * (len(begun) + len(flat)),
        out_specs=[VMEM, VMEM, VMEM],
        out_shape=[jax.ShapeDtypeStruct(shape, jnp.float32), half, half],
        scratch_shapes=[sums]
        + [pltpu.VMEM(array.shape, array.dtype) for array in flat]
        + [pltpu.SemaphoreType.DMA((len(begun) + len(flat),))],
        compiler_params=PARAMS if rows <= 8 else ALONE,
        cost_estimate=cost(4 * rows * high * lanes, 100 * rows * high * lanes),
    )(targets, place, *begun, *flat)


def finish_kernel(*refs):
    terms, out_ref = refs[:-1], refs[-1]
    window = out_ref.shape[2]
    for p in range(out_ref.shape[0] // 2):
        total = sum(
            (term[0, 0, p] if term.ndim == 5 else term[0, p]).astype(jnp.float32) for term in terms
        )
        for u in range(2):
            out_ref[2 * p + u] = total[:, u * window : (u + 1) * window]


def finish(*terms):
    pairs, high, lanes = terms[0].shape[-3:]
    return pl.pallas_call(
        finish_kernel,
        in_specs=[VMEM] * len(terms),
        out_specs=VMEM,
        out_shape=jax.ShapeDtypeStruct((2 * pairs, high, lanes // 2), jnp.float32),
        compiler_params=PARAMS if len(terms[0]) <= 2 else ALONE,
        cost_estimate=cost(pairs * high * lanes, 10 * pairs * high * lanes),
    )(*terms)


def flip(count, bit):
    return [(i, i ^ bit) for i in range(count)]


def exchange(keep, send, axis, count, bit, link):
    terms = [(keep, 1)]
    while True:
        route = flip(count, bit)
        if isinstance(send, tuple):
            odd = lax.ppermute(send[0], axis, route)
            arrived = (lax.ppermute(send[1], axis, route), 1)
        else:
            arrived = (lax.ppermute(send, axis, route), 2)
            odd = arrived[0][1::2]
        bit *= 2
        if bit == count:
            return [term for term, _ in terms] + [arrived[0]]
        leave = sum(term[stride :: 2 * stride].astype(jnp.float32) for term, stride in terms)
        send = (leave + odd.astype(jnp.float32)).astype(link)
        terms = [(term, 2 * stride) for term, stride in terms] + [arrived]


def on_device(
    off_blocks,
    neighbour,
    active,
    diag_blocks,
    diag_inverse,
    tentative,
    aggregate,
    owner_row,
    owner_group,
):
    columns, rows = lax.axis_size("col"), lax.axis_size("row")
    col, row = lax.axis_index("col"), lax.axis_index("row")
    assert columns & (columns - 1) == 0 and columns >= 4
    assert rows & (rows - 1) == 0 and rows >= 8
    link = tentative.dtype
    groups = tentative.shape[0] // (2 * RQ)

    pair_a = flip(columns, 1)
    pair_b = [(i, (i + 1) % columns if i % 2 else (i - 1) % columns) for i in range(columns)]

    bounds = [groups * edge // EDGES[-1] for edge in EDGES]
    spans = list(zip(bounds[:-1], bounds[1:]))

    def both(block):
        near_b = lax.ppermute(block, "col", pair_b)
        near_a = lax.ppermute(block, "col", pair_a)
        return near_a, near_b

    packed = list(pack_rows(tentative, spans[:1]))
    packed += pack_rows(tentative, spans[1:])
    halos = [both(block) for block in packed]
    label_a, label_b = both(aggregate)
    labels = jnp.stack([label_a, aggregate, label_b])
    targets = owner_row[:, 0] * G_DEV + owner_group
    other_targets = lax.ppermute(targets, "row", flip(rows, 1))
    targets = jnp.stack([targets, other_targets])
    side = neighbour // RQ
    side = jnp.where(col % 2 == 0, 2 - side, side)
    table = jnp.where(active != 0, side * RQ + neighbour % RQ, 3 * RQ).T
    place = jnp.stack([col, row])
    labels, targets, table, place = lax.optimization_barrier((labels, targets, table, place))

    fields = []
    for (low, high), (near_a, near_b) in zip(spans, halos):
        field = prolong_rows(
            table, labels, off_blocks, diag_blocks, diag_inverse, tentative, near_a, near_b, low
        )
        fields.append((field, *both(field)))
    parts = []
    for part, ((low, high), (field, near_a, near_b)) in enumerate(zip(spans, fields)):
        keep, send = coarse_rows(
            table, place, off_blocks, diag_blocks, field, near_a, near_b, low, columns
        )
        if part == 0:
            other = lax.ppermute(send, "col", pair_a)
            total = (keep + other.astype(jnp.float32)).astype(link)
        else:
            terms = exchange(keep, send, "col", columns, 1, link)
            total = sum(term[:1].astype(jnp.float32) for term in terms).astype(link)
        other = lax.ppermute(total, "row", flip(rows, 1))
        parts.append((total, other))

    starts = [low for low, _ in spans]
    keep, *send = split_groups(targets, place, None, parts[:1], starts[:1], rows)
    terms = exchange(keep, tuple(send), "row", rows, 2, link)
    blocks = sum(term[0].astype(jnp.float32) for term in terms)
    folded = exchange(blocks[0::2], blocks[1::2].astype(link), "col", columns, 2, link)

    early = gather_groups(targets, place, parts[1:-2], starts[1:-2], rows)
    keep, *send = split_groups(targets, place, early, parts[-2:], starts[-2:], rows)
    return finish(*exchange(keep, tuple(send), "row", rows, 2, link), *folded)


def solution(mesh):
    return jax.shard_map(
        on_device,
        mesh=mesh,
        in_specs=(
            P(("row", "col"), None, None, None),
            P(("row", "col"), None),
            P(("row", "col"), None),
            P(("row", "col"), None, None),
            P(("row", "col"), None, None),
            P(("row", "col"), None, None),
            P(("row", "col")),
            P("row", None),
            P("row"),
        ),
        out_specs=P("row", "col", None),
        check_vma=False,
    )
```

```python
import functools

import jax
import jax.numpy as jnp
from jax import lax
from jax.experimental import pallas as pl
from jax.experimental.pallas import tpu as pltpu
from jax.sharding import PartitionSpec as P


CW = 2
RQ = 2
G_DEV = 8
OMEGA = 0.6

EDGES = (0, 4, 8, 14, 16)
AHEAD = 2
STEP = 2


VMEM = pl.BlockSpec(memory_space=pltpu.VMEM)
SMEM = pl.BlockSpec(memory_space=pltpu.SMEM)
ANY = pl.BlockSpec(memory_space=pl.ANY)
PARAMS = pltpu.CompilerParams(vmem_limit_bytes=25165824)
ALONE = pltpu.CompilerParams(vmem_limit_bytes=67043328)


def step_of(first, count):
    return STEP if count % STEP == 0 and first % STEP == 0 else 1


def cost(flops, moved):
    return pl.CostEstimate(flops=int(flops), bytes_accessed=int(moved), transcendentals=0)


def pack_kernel(first, rows_ref, *outs):
    per = 2 * RQ
    width = rows_ref.shape[2]
    base = per * first
    for out in outs:
        for m in range(out.shape[0]):
            for j in range(per):
                out[m, :, j * width : (j + 1) * width] = rows_ref[base + per * m + j]
        base += per * out.shape[0]


def pack_rows(tentative, spans):
    per = 2 * RQ
    _, high, width = tentative.shape
    first, last = spans[0][0], spans[-1][1]
    whole = first % (last - first) == 0
    block = per * (last - first if whole else last)
    at = first // (last - first) if whole else 0
    counts = [stop - start for start, stop in spans]
    return pl.pallas_call(
        functools.partial(pack_kernel, 0 if whole else first),
        grid=(1,),
        in_specs=[pl.BlockSpec((block, high, width), lambda i: (at, 0, 0))],
        out_specs=[
            pl.BlockSpec((count, high, per * width), lambda i: (0, 0, 0)) for count in counts
        ],
        out_shape=[
            jax.ShapeDtypeStruct((count, high, per * width), tentative.dtype) for count in counts
        ],
        compiler_params=PARAMS if first else ALONE,
        cost_estimate=cost(0, 5 * sum(counts) * per * high * width),
    )(tentative)


def prolong_kernel(first, table, labels, off, diag, inverse, own, near_a, near_b, out, *wides):
    step = len(wides) // 2
    slots, size = off.shape[1], off.shape[2]
    window = CW * size
    base = pl.program_id(0) * step
    start = 2 * RQ * (first + base)

    @pl.when(pl.program_id(0) == 0)
    def _():
        for wide in wides:
            wide[3 * RQ] = jnp.zeros((size, window), wide.dtype)

    for c, wide in enumerate(wides):
        m = c // 2
        for k in range(RQ):
            local = RQ * c + k
            j = local % (2 * RQ)
            lanes = slice(j * size, (j + 1) * size)
            for side, block in enumerate(
                (near_a[base + m, :, lanes], own[local], near_b[base + m, :, lanes])
            ):
                label = labels[side, start + local]
                for w in range(CW):
                    wide[side * RQ + k, :, w * size : (w + 1) * size] = jnp.where(
                        label == w, block, jnp.zeros_like(block)
                    )
    sums = []
    for c, wide in enumerate(wides):
        for k in range(RQ):
            local = RQ * c + k
            total = jnp.dot(diag[local], wide[RQ + k], preferred_element_type=jnp.float32)
            for s in range(slots):
                total += jnp.dot(
                    off[local, s],
                    wide[table[s, start + local]],
                    preferred_element_type=jnp.float32,
                )
            sums.append(total.astype(out.dtype))
    for c, wide in enumerate(wides):
        for k in range(RQ):
            local = RQ * c + k
            change = jnp.dot(inverse[local], sums[local], preferred_element_type=jnp.float32)
            out[2 * base + c, :, k * window : (k + 1) * window] = (
                wide[RQ + k].astype(jnp.float32) - OMEGA * change
            ).astype(out.dtype)


def prolong_rows(table, labels, off, diag, inverse, tentative, near_a, near_b, first):
    per = 2 * RQ
    count = near_a.shape[0]
    slots, size = off.shape[1], off.shape[2]
    window = CW * size
    step = step_of(first, count)

    def rows(i):
        return (i + first // step, 0, 0)

    square = pl.BlockSpec((per * step, size, size), rows)
    return pl.pallas_call(
        functools.partial(prolong_kernel, first),
        grid=(count // step,),
        in_specs=[
            SMEM,
            SMEM,
            pl.BlockSpec((per * step, slots, size, size), lambda i: rows(i) + (0,)),
            square,
            square,
            square,
            VMEM,
            VMEM,
        ],
        out_specs=VMEM,
        out_shape=jax.ShapeDtypeStruct((2 * count, size, RQ * window), tentative.dtype),
        scratch_shapes=[pltpu.VMEM((3 * RQ + 1, size, window), tentative.dtype)] * (2 * step),
        compiler_params=PARAMS,
        cost_estimate=cost(
            2 * count * per * (slots + 2) * size * size * window,
            2 * count * per * (slots + 7) * size * size,
        ),
    )(table, labels, off, diag, inverse, tentative, near_a, near_b)


def coarse_kernel(first, table, place, off, diag, own, near_a, near_b, keep, send, *scratch):
    step = len(scratch) // 6
    slots, size = off.shape[1], off.shape[2]
    window = CW * size
    halves, high = keep.shape[0], keep.shape[2]
    col = place[0]
    base = pl.program_id(0) * step
    start = 2 * RQ * (first + base)
    fields, stiffs, wholes = (scratch[2 * step * i : 2 * step * (i + 1)] for i in range(3))

    @pl.when(pl.program_id(0) == 0)
    def _():
        for field in fields:
            field[3 * RQ] = jnp.zeros((size, window), field.dtype)

    for c, field in enumerate(fields):
        for k in range(RQ):
            lanes = slice(k * window, (k + 1) * window)
            for side, source in enumerate((near_a, own, near_b)):
                field[side * RQ + k] = source[2 * base + c, :, lanes]
    for c, (field, stiff) in enumerate(zip(fields, stiffs)):
        for k in range(RQ):
            local = RQ * c + k
            total = jnp.dot(diag[local], field[RQ + k], preferred_element_type=jnp.float32)
            for s in range(slots):
                total += jnp.dot(
                    off[local, s],
                    field[table[s, start + local]],
                    preferred_element_type=jnp.float32,
                )
            stiff[k * size : (k + 1) * size, :] = total.astype(stiff.dtype)
    for field, stiff, whole in zip(fields, stiffs, wholes):
        left = field[RQ : 2 * RQ].reshape(RQ * size, window)
        block = lax.dot_general(
            left, stiff[...], (((0,), (0,)), ((), ())), preferred_element_type=jnp.float32
        )
        for piece in range(2 * halves):
            whole[piece] = block[piece * high : (piece + 1) * high]
    for c, whole in enumerate(wholes):
        lanes = slice(c % 2 * window, (c % 2 + 1) * window)
        for h in range(halves):
            keep[h, base + c // 2, :, lanes] = whole[col ^ (2 * h)]
            send[h, base + c // 2, :, lanes] = whole[col ^ (2 * h + 1)].astype(send.dtype)


def coarse_rows(table, place, off, diag, own, near_a, near_b, first, columns):
    per = 2 * RQ
    count = own.shape[0] // 2
    slots, size = off.shape[1], off.shape[2]
    window = CW * size
    halves, high = columns // 2, window // columns
    step = step_of(first, count)

    def rows(i):
        return (i + first // step, 0, 0)

    shape = (halves, count, high, 2 * window)
    return pl.pallas_call(
        functools.partial(coarse_kernel, first),
        grid=(count // step,),
        in_specs=[
            SMEM,
            SMEM,
            pl.BlockSpec((per * step, slots, size, size), lambda i: rows(i) + (0,)),
            pl.BlockSpec((per * step, size, size), rows),
            VMEM,
            VMEM,
            VMEM,
        ],
        out_specs=[VMEM, VMEM],
        out_shape=[
            jax.ShapeDtypeStruct(shape, jnp.float32),
            jax.ShapeDtypeStruct(shape, own.dtype),
        ],
        scratch_shapes=[pltpu.VMEM((3 * RQ + 1, size, window), own.dtype)] * (2 * step)
        + [pltpu.VMEM((RQ * size, window), own.dtype)] * (2 * step)
        + [pltpu.VMEM((columns, high, window), jnp.float32)] * (2 * step),
        compiler_params=PARAMS,
        cost_estimate=cost(
            2 * count * per * (slots + 3) * size * size * window,
            2 * count * per * (slots + 12) * size * size,
        ),
    )(table, place, off, diag, own, near_a, near_b)


def add_groups(targets, place, sides, first, sums):
    groups = sums.shape[0] - 1
    window = sums.shape[2]
    row = place[1]
    for side, source in enumerate(sides):

        def one(m, source=source, side=side):
            for u in range(2):
                target = targets[side, 2 * (first + m) + u]
                away = (target // G_DEV) ^ row
                spot = jnp.where(away % 2 == 0, away // 2 * G_DEV + target % G_DEV, groups)
                sums[spot] += source[m, :, u * window : (u + 1) * window].astype(jnp.float32)

        for m in range(source.shape[0]):
            one(m)


def bring(sources, buffers, sems):
    copies = [
        pltpu.make_async_copy(source, buffer, sems.at[i])
        for i, (source, buffer) in enumerate(zip(sources, buffers))
    ]
    for copy in copies:
        copy.start()
    return copies


def gather_kernel(starts, targets, place, *refs):
    count = 2 * len(starts)
    sources, sums, buffers, sems = refs[:count], refs[count], refs[count + 1 : -1], refs[-1]
    copies = bring(sources, buffers, sems)
    sums[...] = jnp.zeros_like(sums)
    for part, first in enumerate(starts):
        for copy in copies[2 * part : 2 * part + 2]:
            copy.wait()
        sides = [buffer.at[0] for buffer in buffers[2 * part : 2 * part + 2]]
        add_groups(targets, place, sides, first, sums)


def gather_groups(targets, place, parts, starts, rows):
    _, _, high, lanes = parts[0][0].shape
    shape = (rows // 2 * G_DEV + 1, high, lanes // 2)
    flat = [array for pair in parts for array in pair]
    total = sum(array.size for array in flat)
    return pl.pallas_call(
        functools.partial(gather_kernel, starts),
        in_specs=[SMEM, SMEM] + [ANY] * len(flat),
        out_specs=VMEM,
        out_shape=jax.ShapeDtypeStruct(shape, jnp.float32),
        scratch_shapes=[pltpu.VMEM(array.shape, array.dtype) for array in flat]
        + [pltpu.SemaphoreType.DMA((len(flat),))],
        compiler_params=PARAMS,
        cost_estimate=cost(total, 4 * total),
    )(targets, place, *flat)


def split_kernel(starts, begun, targets, place, *refs):
    count = 2 * len(starts)
    sources, (keep, odd, even, sums) = refs[: begun + count], refs[begun + count :][:4]
    buffers, sems = refs[begun + count + 4 : -1], refs[-1]
    copies = bring(sources, ((sums,) if begun else ()) + buffers, sems)
    window = sums.shape[2]
    for y in range(keep.shape[1]):
        if not begun:
            sums[...] = jnp.zeros_like(sums)
        if y == 0:
            for copy in copies:
                copy.wait()
        for part, first in enumerate(starts):
            sides = [buffer.at[y] for buffer in buffers[2 * part : 2 * part + 2]]
            add_groups(targets, place, sides, first, sums)
        for h in range(keep.shape[0]):
            send = odd if h % 2 else even
            for p in range(keep.shape[2]):
                for u in range(2):
                    lanes = slice(u * window, (u + 1) * window)
                    inner = 2 * p + u
                    keep[h, y, p, :, lanes] = sums[2 * h * G_DEV + inner]
                    away = sums[(2 * h + 1) * G_DEV + inner]
                    send[h // 2, y, p, :, lanes] = away.astype(send.dtype)


def split_groups(targets, place, early, parts, starts, rows):
    layers, _, high, lanes = parts[0][0].shape
    shape = (rows // 4, layers, G_DEV // 2, high, lanes)
    flat = [array for pair in parts for array in pair]
    half = jax.ShapeDtypeStruct((rows // 8,) + shape[1:], flat[0].dtype)
    sums = pltpu.VMEM((rows // 2 * G_DEV + 1, high, lanes // 2), jnp.float32)
    begun = [] if early is None else [early]
    assert layers == 1 or not begun
    return pl.pallas_call(
        functools.partial(split_kernel, starts, len(begun)),
        in_specs=[SMEM, SMEM] + [ANY] * (len(begun) + len(flat)),
        out_specs=[VMEM, VMEM, VMEM],
        out_shape=[jax.ShapeDtypeStruct(shape, jnp.float32), half, half],
        scratch_shapes=[sums]
        + [pltpu.VMEM(array.shape, array.dtype) for array in flat]
        + [pltpu.SemaphoreType.DMA((len(begun) + len(flat),))],
        compiler_params=PARAMS if rows <= 8 else ALONE,
        cost_estimate=cost(4 * rows * high * lanes, 100 * rows * high * lanes),
    )(targets, place, *begun, *flat)


def finish_kernel(*refs):
    terms, out_ref = refs[:-1], refs[-1]
    window = out_ref.shape[2]
    for p in range(out_ref.shape[0] // 2):
        total = sum(
            (term[0, 0, p] if term.ndim == 5 else term[0, p]).astype(jnp.float32) for term in terms
        )
        for u in range(2):
            out_ref[2 * p + u] = total[:, u * window : (u + 1) * window]


def finish(*terms):
    pairs, high, lanes = terms[0].shape[-3:]
    return pl.pallas_call(
        finish_kernel,
        in_specs=[VMEM] * len(terms),
        out_specs=VMEM,
        out_shape=jax.ShapeDtypeStruct((2 * pairs, high, lanes // 2), jnp.float32),
        compiler_params=PARAMS if len(terms[0]) <= 2 else ALONE,
        cost_estimate=cost(pairs * high * lanes, 10 * pairs * high * lanes),
    )(*terms)


def flip(count, bit):
    return [(i, i ^ bit) for i in range(count)]


def exchange(keep, send, axis, count, bit, link):
    terms = [(keep, 1)]
    while True:
        route = flip(count, bit)
        if isinstance(send, tuple):
            odd = lax.ppermute(send[0], axis, route)
            arrived = (lax.ppermute(send[1], axis, route), 1)
        else:
            arrived = (lax.ppermute(send, axis, route), 2)
            odd = arrived[0][1::2]
        bit *= 2
        if bit == count:
            return [term for term, _ in terms] + [arrived[0]]
        leave = sum(term[stride :: 2 * stride].astype(jnp.float32) for term, stride in terms)
        send = (leave + odd.astype(jnp.float32)).astype(link)
        terms = [(term, 2 * stride) for term, stride in terms] + [arrived]


def on_device(
    off_blocks,
    neighbour,
    active,
    diag_blocks,
    diag_inverse,
    tentative,
    aggregate,
    owner_row,
    owner_group,
):
    columns, rows = lax.axis_size("col"), lax.axis_size("row")
    col, row = lax.axis_index("col"), lax.axis_index("row")
    assert columns & (columns - 1) == 0 and columns >= 4
    assert rows & (rows - 1) == 0 and rows >= 8
    link = tentative.dtype
    groups = tentative.shape[0] // (2 * RQ)

    pair_a = flip(columns, 1)
    pair_b = [(i, (i + 1) % columns if i % 2 else (i - 1) % columns) for i in range(columns)]

    bounds = [groups * edge // EDGES[-1] for edge in EDGES]
    spans = list(zip(bounds[:-1], bounds[1:]))

    def both(block):
        near_b = lax.ppermute(block, "col", pair_b)
        near_a = lax.ppermute(block, "col", pair_a)
        return near_a, near_b

    packed = list(pack_rows(tentative, spans[:1]))
    packed += pack_rows(tentative, spans[1:])
    halos = [both(block) for block in packed]
    label_a, label_b = both(aggregate)
    labels = jnp.stack([label_a, aggregate, label_b])
    targets = owner_row[:, 0] * G_DEV + owner_group
    other_targets = lax.ppermute(targets, "row", flip(rows, 1))
    targets = jnp.stack([targets, other_targets])
    side = neighbour // RQ
    side = jnp.where(col % 2 == 0, 2 - side, side)
    table = jnp.where(active != 0, side * RQ + neighbour % RQ, 3 * RQ).T
    place = jnp.stack([col, row])
    labels, targets, table, place = lax.optimization_barrier((labels, targets, table, place))

    fields = []
    for (low, high), (near_a, near_b) in zip(spans, halos):
        field = prolong_rows(
            table, labels, off_blocks, diag_blocks, diag_inverse, tentative, near_a, near_b, low
        )
        fields.append((field, *both(field)))
    parts = []
    for part, ((low, high), (field, near_a, near_b)) in enumerate(zip(spans, fields)):
        keep, send = coarse_rows(
            table, place, off_blocks, diag_blocks, field, near_a, near_b, low, columns
        )
        if part < AHEAD:
            other = lax.ppermute(send, "col", pair_a)
            total = (keep + other.astype(jnp.float32)).astype(link)
        else:
            terms = exchange(keep, send, "col", columns, 1, link)
            total = sum(term[:1].astype(jnp.float32) for term in terms).astype(link)
        other = lax.ppermute(total, "row", flip(rows, 1))
        parts.append((total, other))

    starts = [low for low, _ in spans]
    keep, *send = split_groups(
        targets, place, None, parts[:AHEAD], starts[:AHEAD], rows
    )
    terms = exchange(keep, tuple(send), "row", rows, 2, link)
    blocks = sum(term[0].astype(jnp.float32) for term in terms)
    folded = exchange(blocks[0::2], blocks[1::2].astype(link), "col", columns, 2, link)

    early = None
    if parts[AHEAD:-2]:
        early = gather_groups(
            targets, place, parts[AHEAD:-2], starts[AHEAD:-2], rows
        )
    keep, *send = split_groups(targets, place, early, parts[-2:], starts[-2:], rows)
    return finish(*exchange(keep, tuple(send), "row", rows, 2, link), *folded)


def solution(mesh):
    return jax.shard_map(
        on_device,
        mesh=mesh,
        in_specs=(
            P(("row", "col"), None, None, None),
            P(("row", "col"), None),
            P(("row", "col"), None),
            P(("row", "col"), None, None),
            P(("row", "col"), None, None),
            P(("row", "col"), None, None),
            P(("row", "col")),
            P("row", None),
            P("row"),
        ),
        out_specs=P("row", "col", None),
        check_vma=False,
    )
```
